32 devices in a mesh: expert: 16 (over z, x, core), tensor: 2 (over y).
Axes of the slice: x: 2, y: 2, z: 4, core: 2. Of those that a mesh axis runs over, the one named last changes fastest.
Arguments:
- tokens: bfloat16 [2048, 2048], P('expert', 'tensor'), may hold values from -6 to 6
- cotangent: bfloat16 [2048, 2048], P('expert', 'tensor'), may hold values from -6 to 6
- route_ids: int32 [2048, 6], P('expert'), may hold values from 0 to 15, all different within a row
- route_weights: float32 [2048, 6], P('expert'), may hold values from 0.05 to 0.5
- shared_gate: bfloat16 [1408, 2048], P('tensor'), may hold values from -0.125 to 0.125
- shared_up: bfloat16 [1408, 2048], P('tensor'), may hold values from -0.125 to 0.125
- shared_down: bfloat16 [1408, 2048], P('tensor'), may hold values from -0.15625 to 0.15625
- expert_gate: bfloat16 [16, 1408, 2048], P('expert', 'tensor'), may hold values from -0.125 to 0.125
- expert_up: bfloat16 [16, 1408, 2048], P('expert', 'tensor'), may hold values from -0.125 to 0.125
- expert_down: bfloat16 [16, 1408, 2048], P('expert', 'tensor'), may hold values from -0.15625 to 0.15625
Outputs:
- layer_output: bfloat16 [2048, 2048], P('expert', 'tensor')
- input_grad: bfloat16 [2048, 2048], P('expert', 'tensor')
The draws below stay inside these ranges and needn't reach their ends.
Inputs may be any that keep to these rules, and one draw needn't show every extreme that they name: `route_ids`: each row names 6 different experts.
All inputs are finite; a program needn't handle non-finite values.
Results may differ from the reference program's by a relative error of at most 0.0051.
Values may be sent and summed in bfloat16 or wider, within the bound.
No kernel may reach another device: no remote copies, remote signals or barrier semaphores. Data moves between devices by JAX's collectives and lax.ppermute only.
A program may use at most 64 MiB of HBM per device.

```python
import math
import jax
import jax.numpy as jnp
from jax import lax

D = 2048
FF = 1408
SF = 1408
TOP = 6
TOK_DEV = 128
EXPERTS = 16
CAP = 24
TOKENS = 2048
N_EXPERT = 16
N_TENSOR = 2


def level_of(rng, dims, pieces, smallest, high):
    level = 1.0
    for dim, blocks in pieces:
        heights = jax.random.uniform(jax.random.fold_in(jax.random.fold_in(rng, 6), dim), (blocks,), jnp.float32, smallest / len(pieces), high / len(pieces))
        level = level * jnp.repeat(jnp.exp(heights), dims[dim] // blocks).reshape((-1,) + (1,) * (len(dims) - 1 - dim))
    return level


def different_ones(stream_key, rows, number_of, top, lift):
    ranking = jax.random.permutation(jax.random.fold_in(stream_key, 1), number_of)
    boost = ranking
    for power in range(3):
        boost = boost * boost // number_of
    boost = boost * lift // number_of
    chance = jax.random.randint(jax.random.fold_in(stream_key, 2), (rows, number_of), 0, 4096) + boost
    fixed_rows = jax.random.permutation(jax.random.fold_in(stream_key, 3), rows)[jnp.arange(number_of) % rows]
    chance = jnp.where(jnp.arange(rows)[:, None] == fixed_rows[None, :], 1 << 14, chance)
    merit = chance * number_of + jnp.arange(number_of)
    return lax.top_k(merit.astype(jnp.int32), top)[1].astype(jnp.int32)


def scatter_about(own_key, extent, scale, most, pieces=(), held_as=jnp.bfloat16):
    array = scale * jax.random.normal(own_key, extent, jnp.float32)
    if pieces:
        array = array * level_of(own_key, extent, pieces, -0.22, 0.18)
    return jnp.clip(array, -most, most).astype(held_as)


def setup_inputs(seed: int = 0) -> dict:
    arg_keys = jax.random.split(jax.random.key(seed), 11)
    return {
        "tokens": scatter_about(arg_keys[0], (TOKENS, D), 1.0, 6.0, ((0, 16), (1, 2))),
        "cotangent": scatter_about(arg_keys[1], (TOKENS, D), 1.0, 6.0, ((0, 16), (1, 2))),
        "route_ids": different_ones(arg_keys[2], TOKENS, EXPERTS, TOP, 6144),
        "route_weights": jnp.clip(jnp.exp(math.log(0.5) - 2.3025851 * jax.random.uniform(arg_keys[3], (TOKENS, TOP), jnp.float32) ** level_of(arg_keys[3], (TOKENS, TOP), ((0, 16),), -0.2, 0.2)), 0.05, 0.5),
        "shared_gate": scatter_about(arg_keys[4], (SF, D), D ** -0.5, 0.125, ((0, 2),)),
        "shared_up": scatter_about(arg_keys[5], (SF, D), D ** -0.5, 0.125, ((0, 2),)),
        "shared_down": scatter_about(arg_keys[6], (SF, D), SF ** -0.5, 0.15625, ((0, 2),)),
        "expert_gate": scatter_about(arg_keys[7], (EXPERTS, FF, D), D ** -0.5, 0.125, ((0, 16), (1, 2))),
        "expert_up": scatter_about(arg_keys[8], (EXPERTS, FF, D), D ** -0.5, 0.125, ((0, 16), (1, 2))),
        "expert_down": scatter_about(arg_keys[9], (EXPERTS, FF, D), FF ** -0.5, 0.15625, ((0, 16), (1, 2))),
    }


def silu_parts(pre_act):
    sigmoid_value = jax.nn.sigmoid(pre_act)
    return pre_act * sigmoid_value, sigmoid_value * (1.0 + pre_act * (1.0 - sigmoid_value))


def round_trip(values):
    return lax.optimization_barrier(values.astype(jnp.bfloat16)).astype(jnp.float32)


def reference(tokens, cotangent, route_ids, route_weights, shared_gate, shared_up, shared_down, expert_gate, expert_up, expert_down):
    per_block = TOK_DEV * TOP
    rows_expert = N_EXPERT * CAP
    flat_ids = route_ids.reshape(N_EXPERT, per_block).astype(jnp.int32)
    expert_ids = jnp.arange(EXPERTS, dtype=jnp.int32)
    one_hot = (flat_ids[:, :, None] == expert_ids[None, None, :]).astype(jnp.int32)
    rank_in = jnp.sum((jnp.cumsum(one_hot, axis=1) - one_hot) * one_hot, axis=2).astype(jnp.int32)
    block_ids = jnp.arange(N_EXPERT, dtype=jnp.int32)[:, None]
    flat_pos = block_ids * per_block + jnp.arange(per_block, dtype=jnp.int32)[None, :]
    target = jnp.where(rank_in < CAP, flat_ids * rows_expert + block_ids * CAP + rank_in, EXPERTS * rows_expert).astype(jnp.int32)
    slot_table = jnp.full((EXPERTS * rows_expert,), -1, jnp.int32).at[target.reshape(-1)].set(flat_pos.reshape(-1).astype(jnp.int32), mode="drop")
    slot_table = slot_table.reshape(EXPERTS, rows_expert)
    gate_flat = route_weights.reshape(-1)
    group_width = FF // N_TENSOR

    def expert_step(carried, inputs):
        out_total, grad_total = carried
        positions, w_gate, w_up, w_down = inputs
        valid_row = positions >= 0
        safe_pos = jnp.maximum(positions, 0).astype(jnp.int32)
        token_ids = (safe_pos // TOP).astype(jnp.int32)
        zero_bf = jnp.zeros((), jnp.bfloat16)
        x_rows = jnp.where(valid_row[:, None], tokens[token_ids], zero_bf)
        c_rows = jnp.where(valid_row[:, None], cotangent[token_ids], zero_bf)
        weights = jnp.where(valid_row, gate_flat[safe_pos], jnp.zeros((), jnp.float32)).astype(jnp.float32)
        grad_rows = (weights[:, None] * c_rows.astype(jnp.float32)).astype(jnp.bfloat16)
        gate_pre = jnp.dot(x_rows, w_gate.T, preferred_element_type=jnp.float32)
        up_pre = jnp.dot(x_rows, w_up.T, preferred_element_type=jnp.float32)
        act_value, act_slope = silu_parts(gate_pre)
        hidden = (act_value * up_pre).astype(jnp.bfloat16)
        grad_hidden = jnp.dot(grad_rows, w_down.T, preferred_element_type=jnp.float32)
        grad_gate = (grad_hidden * up_pre * act_slope).astype(jnp.bfloat16)
        grad_up = (grad_hidden * act_value).astype(jnp.bfloat16)
        value_sum = jnp.zeros((rows_expert, D), jnp.float32)
        input_sum = jnp.zeros((rows_expert, D), jnp.float32)
        for group_index in range(N_TENSOR):
            low_col = group_index * group_width
            high_col = low_col + group_width
            value_sum = value_sum + round_trip(jnp.dot(hidden[:, low_col:high_col], w_down[low_col:high_col], preferred_element_type=jnp.float32))
            input_term = jnp.dot(grad_gate[:, low_col:high_col], w_gate[low_col:high_col], preferred_element_type=jnp.float32)
            input_term = input_term + jnp.dot(grad_up[:, low_col:high_col], w_up[low_col:high_col], preferred_element_type=jnp.float32)
            input_sum = input_sum + round_trip(input_term)
        dest_row = jnp.where(valid_row, token_ids, TOKENS).astype(jnp.int32)
        out_total = out_total.at[dest_row].add(weights[:, None] * value_sum, mode="drop")
        grad_total = grad_total.at[dest_row].add(input_sum, mode="drop")
        return (out_total, grad_total), None

    initial = (jnp.zeros((TOKENS, D), jnp.float32), jnp.zeros((TOKENS, D), jnp.float32))
    (routed_out, routed_grad), unused = lax.scan(expert_step, initial, (slot_table, expert_gate, expert_up, expert_down))

    shared_gate_pre = jnp.dot(tokens, shared_gate.T, preferred_element_type=jnp.float32)
    shared_up_pre = jnp.dot(tokens, shared_up.T, preferred_element_type=jnp.float32)
    shared_act, shared_slope = silu_parts(shared_gate_pre)
    shared_hidden = (shared_act * shared_up_pre).astype(jnp.bfloat16)
    shared_value = jnp.dot(shared_hidden, shared_down, preferred_element_type=jnp.float32)
    shared_grad_hidden = jnp.dot(cotangent, shared_down.T, preferred_element_type=jnp.float32)
    shared_grad_gate = (shared_grad_hidden * shared_up_pre * shared_slope).astype(jnp.bfloat16)
    shared_grad_up = (shared_grad_hidden * shared_act).astype(jnp.bfloat16)
    shared_input = jnp.dot(shared_grad_gate, shared_gate, preferred_element_type=jnp.float32)
    shared_input = shared_input + jnp.dot(shared_grad_up, shared_up, preferred_element_type=jnp.float32)
    return ((shared_value + routed_out).astype(jnp.bfloat16), (shared_input + routed_grad).astype(jnp.bfloat16))
```

```python
import functools
import math

import jax
import jax.numpy as jnp
from jax import lax
from jax.experimental import pallas as pl
from jax.experimental.pallas import tpu as pltpu
from jax.sharding import PartitionSpec as P


BF = jnp.bfloat16
F32 = jnp.float32
ROWS_BY_ROWS = (((1,), (1,)), ((), ()))


def silu_parts(pre_act):
    sigmoid_value = jax.nn.sigmoid(pre_act)
    return (pre_act * sigmoid_value, sigmoid_value * (1.0 + pre_act * (1.0 - sigmoid_value)))


def mm(a, b):
    return jnp.dot(a, b, preferred_element_type=F32)


def mmt(a, b):
    return lax.dot_general(a, b, ROWS_BY_ROWS, preferred_element_type=F32)


def local_call(body, scalars, arrays, outs, name, flops=0, scratch=(), staged=None):
    staged = len(arrays) if staged is None else staged
    count = len(arrays)

    def kernel(*refs):
        scalar_ref, ins = refs[0], refs[1 : count + 1]
        out_refs = refs[count + 1 : count + 1 + len(outs)]
        rest = refs[count + 1 + len(outs) :]
        bufs, sem, extra = rest[:staged], rest[staged], rest[staged + 1 :]
        copies = [
            pltpu.make_async_copy(ins[i], bufs[i], sem.at[i]) for i in range(staged)
        ]
        for copy in copies:
            copy.start()

        def ready(*which):
            for i in which:
                copies[i].wait()

        body(scalar_ref, bufs, ins[staged:], out_refs, extra, ready)

    moved = sum(math.prod(a.shape) * a.dtype.itemsize for a in arrays)
    moved += sum(math.prod(o.shape) * o.dtype.itemsize for o in outs)
    return pl.pallas_call(
        kernel,
        out_shape=list(outs),
        in_specs=[pl.BlockSpec(memory_space=pltpu.SMEM)]
        + [pl.BlockSpec(memory_space=pl.ANY)] * count,
        out_specs=[pl.BlockSpec(memory_space=pltpu.VMEM)] * len(outs),
        scratch_shapes=[pltpu.VMEM(a.shape, a.dtype) for a in arrays[:staged]]
        + [pltpu.SemaphoreType.DMA((staged,))]
        + list(scratch),
        compiler_params=pltpu.CompilerParams(vmem_limit_bytes=40 << 20),
        cost_estimate=pl.CostEstimate(flops=flops, bytes_accessed=moved, transcendentals=0),
        name=name,
    )(scalars, *arrays)


def shaped(shape, dtype=BF):
    return jax.ShapeDtypeStruct(shape, dtype)


def prep(scalars, ids_t, wts_t, tokens, cotangent, experts, cap):
    tok_rows, half = tokens.shape
    top_count = ids_t.shape[0]
    slots = experts * cap
    far = experts // 2 - 2

    def body(scalar_ref, bufs, _, outs, extra, ready):
        ids_ref, wts_ref, tok_ref, cot_ref = bufs
        own_out, core_out, dm_out, gm_out = outs
        row = lax.broadcasted_iota(jnp.int32, (slots, 1), 0)
        k = ((row.astype(F32) + 0.5) * (1.0 / cap)).astype(jnp.int32)
        place = (row - k * cap).astype(F32)
        expert = jnp.bitwise_xor(k, scalar_ref[0])
        before = lax.broadcasted_iota(jnp.int32, (tok_rows, tok_rows), 0)
        after = lax.broadcasted_iota(jnp.int32, (tok_rows, tok_rows), 1)
        earlier = jnp.where(before < after, 1.0, 0.0).astype(BF)
        ready(0, 1)
        named = jnp.zeros((slots, tok_rows), F32)
        gate = jnp.zeros((slots, tok_rows), F32)
        for i in range(top_count):
            hit = ids_ref[i : i + 1, :] == expert
            named = jnp.where(hit, 1.0, named)
            gate = jnp.where(hit, wts_ref[i : i + 1, :], gate)
        rank = mm(named.astype(BF), earlier)
        kept = (named > 0.5) & (rank == place)
        dm = jnp.where(kept, 1.0, 0.0)
        gm = jnp.where(kept, gate, 0.0)
        dmb = dm.astype(BF)
        slot_gate = jnp.sum(gm, axis=1, keepdims=True)
        dm_out[...] = dmb
        gm_out[...] = gm
        first = 4 * cap
        ready(2)
        x_rows = mm(dmb[first:], tok_ref[...])
        ready(3)
        g_rows = slot_gate[first:] * mm(dmb[first:], cot_ref[...])
        for q in range(far):
            for b, out in enumerate((own_out, core_out)):
                low = (2 * q + b) * cap
                both = jnp.concatenate((x_rows[low : low + cap], g_rows[low : low + cap]), 0)
                out[2 * cap * q : 2 * cap * (q + 1), :] = both.astype(BF)

    return local_call(
        body,
        scalars,
        (ids_t, wts_t, tokens, cotangent),
        (
            shaped((far * 2 * cap, half)),
            shaped((far * 2 * cap, half)),
            shaped((slots, tok_rows)),
            shaped((slots, tok_rows), F32),
        ),
        "prep",
        flops=4 * slots * tok_rows * half,
    )


def merge_far(scalars, own, core, cap):
    half = own.shape[1]
    far = own.shape[0] // (2 * cap)

    def body(_, bufs, __, outs, extra, ready):
        ready(0, 1)
        for q in range(far):
            for b in range(2):
                outs[q][2 * cap * b : 2 * cap * (b + 1), :] = bufs[b][
                    2 * cap * q : 2 * cap * (q + 1), :
                ]

    return local_call(
        body, scalars, (own, core), [shaped((4 * cap, half))] * far, "merge_far"
    )


def gate_tables(scalars, dm, gm, cap):
    slots, tok_rows = dm.shape
    near = 4 * cap

    def body(_, bufs, __, outs, extra, ready):
        ready(0, 1)
        for out, low, high in ((outs[0], 0, near), (outs[1], near, slots)):
            out[0] = jnp.transpose(bufs[0][low:high, :].astype(F32)).astype(BF)
            gate = jnp.transpose(bufs[1][low:high, :])
            one = gate.astype(BF)
            left = gate - one.astype(F32)
            two = left.astype(BF)
            out[1] = one
            out[2] = two
            out[3] = (left - two.astype(F32)).astype(BF)

    return local_call(
        body,
        scalars,
        (dm, gm),
        (shaped((4, tok_rows, near)), shaped((4, tok_rows, slots - near))),
        "gate_tables",
    )


def near_rows(scalars, dm, gm, tokens, tokens_other, cotangent, cotangent_other, cap):
    tok_rows, half = tokens.shape
    near = 4 * cap

    def body(_, bufs, __, outs, extra, ready):
        dm_ref, gm_ref, t_own, t_oth, c_own, c_oth = bufs
        ready(0, 1)
        dmb = dm_ref[0:near, :]
        slot_gate = jnp.sum(gm_ref[0:near, :], axis=1, keepdims=True)
        ready(2, 3, 4, 5)
        for h, (t_ref, c_ref) in enumerate(((t_own, c_own), (t_oth, c_oth))):
            x_rows = mm(dmb, t_ref[...])
            g_rows = slot_gate * mm(dmb, c_ref[...])
            for q in range(2):
                for b in range(2):
                    low = (2 * q + b) * cap
                    both = jnp.concatenate((x_rows[low : low + cap], g_rows[low : low + cap]), 0)
                    outs[b][q, h] = both.astype(BF)

    return local_call(
        body,
        scalars,
        (dm, gm, tokens, tokens_other, cotangent, cotangent_other),
        [shaped((2, 2, 2 * cap, half))] * 2,
        "near_rows",
        flops=8 * near * tok_rows * half,
    )


def ffn(xs, gs, pieces, ready):
    gate_w, up_w, down_w = pieces[0:2], pieces[2:4], pieces[4:6]
    ready(0)
    gate_pre = mmt(xs[0], gate_w[0][...])
    ready(1)
    gate_pre += mmt(xs[1], gate_w[1][...])
    ready(2)
    up_pre = mmt(xs[0], up_w[0][...])
    ready(3)
    up_pre += mmt(xs[1], up_w[1][...])
    act, slope = silu_parts(gate_pre)
    hidden = (act * up_pre).astype(BF)
    ready(4)
    grad_hidden = mmt(gs[0], down_w[0][...])
    ready(5)
    grad_hidden += mmt(gs[1], down_w[1][...])
    grad_gate = (grad_hidden * up_pre * slope).astype(BF)
    grad_up = (grad_hidden * act).astype(BF)
    values = [mm(hidden, down_w[i][...]) for i in range(2)]
    inputs = [mm(grad_gate, gate_w[i][...]) + mm(grad_up, up_w[i][...]) for i in range(2)]
    return values, inputs


def fetch(scalar_ref, weights, buf, sem):
    half = buf.shape[-1]
    copies = []
    for w in range(3):
        for i in range(2):
            off = pl.multiple_of(jnp.bitwise_xor(scalar_ref[1], i) * half, half)
            copies.append(
                pltpu.make_async_copy(
                    weights[w].at[:, pl.ds(off, half)], buf.at[2 * w + i], sem.at[2 * w + i]
                )
            )
    for copy in copies:
        copy.start()
    return copies


def weight_scratch(weights, half):
    return [
        pltpu.VMEM((6, weights[0].shape[0], half), BF),
        pltpu.SemaphoreType.DMA((6,)),
    ]


def ffn_flops(rows, weights):
    return 12 * rows * weights[0].shape[0] * weights[0].shape[1]


def routed_ffn(scalars, near, far, weights, cap, name):
    half = weights[0].shape[1] // 2
    arrays = list(near) + [a for pair in far for a in pair]
    staged = len(arrays)
    count = len(near) + len(far)

    def body(scalar_ref, bufs, weight_refs, outs, extra, ready):
        buf, sem = extra
        copies = fetch(scalar_ref, weight_refs, buf, sem)
        ready(*range(staged))

        def views(refs):
            pairs = [(r.at[0], r.at[1]) for r in refs[: len(near)]]
            rest = refs[len(near) :]
            return pairs + [(rest[2 * i], rest[2 * i + 1]) for i in range(len(far))]

        def pick(h, part):
            segments = []
            for pair in views(bufs):
                block = pair[h][...].astype(F32)
                for b in range(2):
                    low = (2 * b + part) * cap
                    segments.append(block[low : low + cap])
            return jnp.concatenate(segments, 0).astype(BF)

        xs = [pick(0, 0), pick(1, 0)]
        gs = [pick(0, 1), pick(1, 1)]
        values, inputs = ffn(xs, gs, [buf.at[i] for i in range(6)], lambda i: copies[i].wait())
        for n, pair in enumerate(views(outs)):
            for h in range(2):
                segments = []
                for b in range(2):
                    low = (2 * n + b) * cap
                    segments += [values[h][low : low + cap], inputs[h][low : low + cap]]
                pair[h][...] = jnp.concatenate(segments, 0).astype(BF)

    outs = local_call(
        body,
        scalars,
        arrays + list(weights),
        [shaped(a.shape) for a in arrays],
        name,
        flops=ffn_flops(2 * cap * count, weights),
        scratch=weight_scratch(weights, half),
        staged=staged,
    )
    rest = outs[len(near) :]
    return outs[: len(near)], [(rest[2 * i], rest[2 * i + 1]) for i in range(len(far))]


def shared_ffn(scalars, tokens, tokens_other, cotangent, cotangent_other, weights):
    tok_rows, half = tokens.shape

    def body(scalar_ref, bufs, weight_refs, outs, extra, ready):
        buf, sem = extra
        copies = fetch(scalar_ref, weight_refs, buf, sem)
        ready(0, 1, 2, 3)
        xs = [bufs[0][...], bufs[1][...]]
        gs = [bufs[2][...], bufs[3][...]]
        values, inputs = ffn(xs, gs, [buf.at[i] for i in range(6)], lambda i: copies[i].wait())
        for h in range(2):
            outs[h][0] = values[h]
            outs[h][1] = inputs[h]

    return local_call(
        body,
        scalars,
        (tokens, tokens_other, cotangent, cotangent_other, *weights),
        [shaped((2, tok_rows, half), F32)] * 2,
        "shared_ffn",
        flops=ffn_flops(tok_rows, weights),
        scratch=weight_scratch(weights, half),
        staged=4,
    )


def combine(table, segments, cap):
    values = jnp.concatenate([s[:cap] for s in segments], 0).astype(BF)
    inputs = jnp.concatenate([s[cap:] for s in segments], 0).astype(BF)
    value = mm(table[1], values) + mm(table[2], values) + mm(table[3], values)
    return value, mm(table[0], inputs)


def near_combine(scalars, table, own0, own1, core0, core1, shared_own, shared_other, cap):
    _, tok_rows, half = shared_own.shape

    def body(_, bufs, __, outs, extra, ready):
        table_ref, own0_ref, own1_ref, core0_ref, core1_ref, s_own, s_oth = bufs
        ready(*range(7))
        for h, shared in enumerate((s_own, s_oth)):
            segments = []
            for own, core in ((own0_ref, core0_ref), (own1_ref, core1_ref)):
                segments.append(own[h].astype(F32)[: 2 * cap])
                segments.append(core[h].astype(F32)[2 * cap :])
            value, grad = combine(table_ref, segments, cap)
            if h == 0:
                outs[0][0] = shared[0] + value
                outs[0][1] = shared[1] + grad
            else:
                outs[1][0] = (shared[0] + value).astype(BF)
                outs[1][1] = (shared[1] + grad).astype(BF)

    return local_call(
        body,
        scalars,
        (table, own0, own1, core0, core1, shared_own, shared_other),
        (shaped((2, tok_rows, half), F32), shaped((2, tok_rows, half))),
        "near_combine",
        flops=16 * tok_rows * 4 * cap * half,
    )


def far_combine(scalars, table, base, partner, own, core, cap):
    _, tok_rows, half = base.shape
    far = len(own)

    def body(_, bufs, __, outs, extra, ready):
        table_ref, base_ref, partner_ref = bufs[:3]
        blocks = bufs[3:]
        ready(*range(3 + 2 * far))
        segments = []
        for q in range(far):
            segments.append(blocks[q][...].astype(F32)[: 2 * cap])
            segments.append(blocks[far + q][...].astype(F32)[2 * cap :])
        value, grad = combine(table_ref, segments, cap)
        outs[0][...] = (base_ref[0] + partner_ref[0].astype(F32) + value).astype(BF)
        outs[1][...] = (base_ref[1] + partner_ref[1].astype(F32) + grad).astype(BF)

    return local_call(
        body,
        scalars,
        (table, base, partner, *own, *core),
        [shaped((tok_rows, half))] * 2,
        "far_combine",
        flops=8 * tok_rows * 2 * far * cap * half,
    )


def paired(
    tokens,
    cotangent,
    route_ids,
    route_weights,
    shared_gate,
    shared_up,
    shared_down,
    expert_gate,
    expert_up,
    expert_down,
):
    experts = lax.axis_size("expert")
    tok_rows, top_count = route_ids.shape
    cap = tok_rows * top_count // (2 * experts)
    scalars = jnp.stack([lax.axis_index("expert"), lax.axis_index("tensor")]).astype(jnp.int32)
    routed = (expert_gate[0], expert_up[0], expert_down[0])
    shared = (shared_gate, shared_up, shared_down)

    def across(values):
        return lax.ppermute(values, "tensor", [(0, 1), (1, 0)])

    def exchange(values, k):
        return lax.ppermute(values, "expert", [(i, i ^ k) for i in range(experts)])

    tokens_other = across(tokens)
    cotangent_other = across(cotangent)
    own_far, core_far, dm, gm = prep(
        scalars, route_ids.T, route_weights.T, tokens, cotangent, experts, cap
    )
    merged = merge_far(scalars, own_far, exchange(core_far, 1), cap)
    chips = experts // 2
    far_order = list(range(chips // 2, chips)) + list(range(2, chips // 2))
    arrived = {q: exchange(merged[q - 2], 2 * q) for q in far_order}
    near_table, far_table = gate_tables(scalars, dm, gm, cap)
    near_own, near_core = near_rows(
        scalars, dm, gm, tokens, tokens_other, cotangent, cotangent_other, cap
    )
    near_back = exchange(near_core, 1)
    near0 = jnp.concatenate((near_own[0], near_back[0]), axis=1)
    near1 = exchange(jnp.concatenate((near_own[1], near_back[1]), axis=1), 2)
    shared_own, shared_other = shared_ffn(
        scalars, tokens, tokens_other, cotangent, cotangent_other, shared
    )
    returned = {}

    def far_group(group):
        pairs = [(arrived[q], across(arrived[q])) for q in group]
        _, results = routed_ffn(scalars, (), pairs, routed, cap, "far_ffn")
        for q, (own, other) in zip(group, results):
            total = (own.astype(F32) + across(other).astype(F32)).astype(BF)
            returned[q] = exchange(total, 2 * q)

    (out0, out1), _ = routed_ffn(scalars, (near0, near1), (), routed, cap, "near_ffn")
    home1 = exchange(out1, 2)
    base, partial = near_combine(
        scalars,
        near_table,
        out0,
        home1,
        exchange(out0, 1),
        exchange(home1, 1),
        shared_own,
        shared_other,
        cap,
    )
    partner = across(partial)
    for low in range(0, len(far_order), 2):
        far_group(far_order[low : low + 2])
    own = [returned[q] for q in range(2, chips)]
    core = [exchange(block, 1) for block in own]
    return far_combine(scalars, far_table, base, partner, own, core, cap)


def serves(mesh_shape, args):
    tokens, _, route_ids = args[:3]
    experts, tensor = mesh_shape["expert"], mesh_shape["tensor"]
    block, top_count = route_ids.shape[0] // experts, route_ids.shape[1]
    cap = block * top_count // (2 * experts)
    return (
        tensor == 2
        and args[7].shape[0] == experts
        and experts >= 8
        and experts & (experts - 1) == 0
        and cap % 8 == 0
        and block % 16 == 0
    )


def on_device(
    tokens,
    cotangent,
    route_ids,
    route_weights,
    shared_gate,
    shared_up,
    shared_down,
    expert_gate,
    expert_up,
    expert_down,
):
    expert_count = lax.axis_size("expert")
    tok_rows, top_count = route_ids.shape
    local_experts = expert_gate.shape[0]
    all_experts = local_experts * expert_count
    capacity = tok_rows * top_count // (2 * all_experts)
    slot_total = all_experts * capacity
    flat_ids = route_ids.reshape(-1)
    one_hot = (flat_ids[:, None] == jnp.arange(all_experts, dtype=jnp.int32)[None, :]).astype(
        jnp.int32
    )
    rank_in = jnp.sum((jnp.cumsum(one_hot, axis=0) - one_hot) * one_hot, axis=1)
    kept_mask = rank_in < capacity
    slot_index = jnp.where(kept_mask, flat_ids * capacity + rank_in, slot_total)
    slot_match = jnp.arange(slot_total, dtype=jnp.int32)[:, None] == slot_index[None, :]
    dispatch = jnp.any(slot_match.reshape(slot_total, tok_rows, top_count), axis=2).astype(
        jnp.bfloat16
    )
    gate_flat = route_weights.reshape(-1)
    slot_gate = jnp.sum(jnp.where(slot_match, gate_flat[None, :], 0.0), axis=1)
    gate_dispatch = dispatch.astype(jnp.float32) * slot_gate[:, None]
    x_full, c_full = (
        lax.all_gather(tokens, "tensor", axis=1, tiled=True),
        lax.all_gather(cotangent, "tensor", axis=1, tiled=True),
    )
    x_slots = jnp.dot(dispatch, tokens, preferred_element_type=jnp.float32).astype(jnp.bfloat16)
    g_slots = (
        slot_gate[:, None] * jnp.dot(dispatch, cotangent, preferred_element_type=jnp.float32)
    ).astype(jnp.bfloat16)
    x_part, g_part = (
        lax.all_to_all(x_slots, "expert", split_axis=0, concat_axis=0, tiled=True),
        lax.all_to_all(g_slots, "expert", split_axis=0, concat_axis=0, tiled=True),
    )
    x_recv, g_recv = (
        lax.all_gather(x_part, "tensor", axis=1, tiled=True),
        lax.all_gather(g_part, "tensor", axis=1, tiled=True),
    )

    def owner_layout(values):
        shaped = values.reshape(expert_count, local_experts, capacity, values.shape[-1])
        return shaped.transpose(1, 0, 2, 3).reshape(
            local_experts, expert_count * capacity, values.shape[-1]
        )

    def source_layout(values):
        shaped = values.reshape(local_experts, expert_count, capacity, values.shape[-1])
        return shaped.transpose(1, 0, 2, 3).reshape(slot_total, values.shape[-1])

    x_own = owner_layout(x_recv)
    g_own = owner_layout(g_recv)
    gate_pre = jnp.einsum("erd,efd->erf", x_own, expert_gate, preferred_element_type=jnp.float32)
    up_pre = jnp.einsum("erd,efd->erf", x_own, expert_up, preferred_element_type=jnp.float32)
    act_value, act_slope = silu_parts(gate_pre)
    hidden = (act_value * up_pre).astype(jnp.bfloat16)
    grad_hidden = jnp.einsum("erd,efd->erf", g_own, expert_down, preferred_element_type=jnp.float32)
    grad_gate = (grad_hidden * up_pre * act_slope).astype(jnp.bfloat16)
    grad_up = (grad_hidden * act_value).astype(jnp.bfloat16)
    value_part = source_layout(
        jnp.einsum("erf,efd->erd", hidden, expert_down, preferred_element_type=jnp.float32).astype(
            jnp.bfloat16
        )
    )
    grads_joined = jnp.concatenate((grad_gate, grad_up), axis=2)
    weights_joined = jnp.concatenate((expert_gate, expert_up), axis=1)
    input_term = jnp.einsum(
        "erf,efd->erd", grads_joined, weights_joined, preferred_element_type=jnp.float32
    )
    input_part = source_layout(input_term.astype(jnp.bfloat16))
    shared_gate_pre = jnp.einsum(
        "td,fd->tf", x_full, shared_gate, preferred_element_type=jnp.float32
    )
    shared_up_pre = jnp.einsum("td,fd->tf", x_full, shared_up, preferred_element_type=jnp.float32)
    shared_act, shared_slope = silu_parts(shared_gate_pre)
    shared_hidden = (shared_act * shared_up_pre).astype(jnp.bfloat16)
    shared_value = jnp.dot(shared_hidden, shared_down, preferred_element_type=jnp.float32)
    shared_grad_hidden = jnp.einsum(
        "td,fd->tf", c_full, shared_down, preferred_element_type=jnp.float32
    )
    shared_grad_gate = (shared_grad_hidden * shared_up_pre * shared_slope).astype(jnp.bfloat16)
    shared_grad_up = (shared_grad_hidden * shared_act).astype(jnp.bfloat16)
    shared_input = jnp.dot(shared_grad_gate, shared_gate, preferred_element_type=jnp.float32)
    shared_input = shared_input + jnp.dot(
        shared_grad_up, shared_up, preferred_element_type=jnp.float32
    )
    value_back, input_back = (
        lax.all_to_all(value_part, "expert", split_axis=0, concat_axis=0, tiled=True),
        lax.all_to_all(input_part, "expert", split_axis=0, concat_axis=0, tiled=True),
    )
    early_value = shared_value + jnp.einsum(
        "st,sd->td",
        gate_dispatch,
        value_back.astype(jnp.float32),
        precision=lax.Precision.HIGHEST,
        preferred_element_type=jnp.float32,
    )
    early_input = shared_input + jnp.einsum(
        "st,sd->td",
        dispatch,
        input_back,
        precision=lax.Precision.HIGHEST,
        preferred_element_type=jnp.float32,
    )
    value_total, input_total = (
        lax.psum_scatter(early_value, "tensor", scatter_dimension=1, tiled=True),
        lax.psum_scatter(early_input, "tensor", scatter_dimension=1, tiled=True),
    )
    return (value_total.astype(jnp.bfloat16), input_total.astype(jnp.bfloat16))


def solution(mesh):
    in_specs = (
        P("expert", "tensor"),
        P("expert", "tensor"),
        P("expert", None),
        P("expert", None),
        P("tensor", None),
        P("tensor", None),
        P("tensor", None),
        P("expert", "tensor", None),
        P("expert", "tensor", None),
        P("expert", "tensor", None),
    )
    out_specs = (P("expert", "tensor"), P("expert", "tensor"))

    def layer(*args):
        program = paired if serves(dict(mesh.shape), args) else on_device
        return jax.shard_map(
            program, mesh=mesh, in_specs=in_specs, out_specs=out_specs, check_vma=False
        )(*args)

    return layer
```

```python
import math

import jax
import jax.numpy as jnp
from jax import lax
from jax.experimental import pallas as pl
from jax.experimental.pallas import tpu as pltpu
from jax.sharding import PartitionSpec as P


BF = jnp.bfloat16
F32 = jnp.float32
ROWS_BY_ROWS = (((1,), (1,)), ((), ()))


def silu_parts(pre_act):
    sigmoid_value = jax.nn.sigmoid(pre_act)
    return (pre_act * sigmoid_value, sigmoid_value * (1.0 + pre_act * (1.0 - sigmoid_value)))


def mm(a, b):
    return jnp.dot(a, b, preferred_element_type=F32)


def mmt(a, b):
    return lax.dot_general(a, b, ROWS_BY_ROWS, preferred_element_type=F32)


def local_call(body, scalars, arrays, outs, flops=0, staged=0, grant=20, keep=0):
    count = len(arrays)

    def kernel(*refs):
        scalar_ref, ins = refs[0], refs[1 : count + 1]
        out_refs = refs[count + 1 : count + 1 + len(outs)]
        sem = refs[-1]
        bufs = list(refs[count + 1 + len(outs) :][: staged - keep])
        bufs += out_refs[len(outs) - keep :] if keep else ()
        copies = [pltpu.make_async_copy(ins[i], bufs[i], sem.at[i]) for i in range(staged)]
        for copy in copies:
            copy.start()

        def ready(*which):
            for i in which:
                copies[i].wait()

        body(scalar_ref, bufs + list(ins[staged:]), out_refs, ready)

    arrays = [
        pltpu.with_memory_space_constraint(a, pltpu.HBM) if i < staged else a
        for i, a in enumerate(arrays)
    ]
    moved = sum(math.prod(a.shape) * a.dtype.itemsize for a in arrays)
    moved += sum(math.prod(o.shape) * o.dtype.itemsize for o in outs)
    whole = pl.BlockSpec(memory_space=pltpu.VMEM)
    return pl.pallas_call(
        kernel,
        out_shape=list(outs),
        in_specs=[pl.BlockSpec(memory_space=pltpu.SMEM)]
        + [pl.BlockSpec(memory_space=pltpu.HBM)] * staged
        + [whole] * (count - staged),
        out_specs=[whole] * len(outs),
        scratch_shapes=[pltpu.VMEM(a.shape, a.dtype) for a in arrays[: staged - keep]]
        + [pltpu.SemaphoreType.DMA((max(staged, 1),))],
        compiler_params=pltpu.CompilerParams(vmem_limit_bytes=grant << 20),
        cost_estimate=pl.CostEstimate(flops=flops, bytes_accessed=moved, transcendentals=0),
    )(scalars, *arrays)


def shaped(shape, dtype=BF):
    return jax.ShapeDtypeStruct(shape, dtype)


def prep(scalars, ids_t, wts_t, tokens, cotangent, experts, cap, near_chips):
    tok_rows, half = tokens.shape
    top_count = ids_t.shape[0]
    slots = experts * cap
    far = experts // 2 - near_chips

    def body(scalar_ref, bufs, outs, ready):
        ids_ref, wts_ref, tok_ref, cot_ref = bufs
        core_out, dm_out, gm_out = outs[far : far + 3]
        row = lax.broadcasted_iota(jnp.int32, (slots, 1), 0)
        k = ((row.astype(F32) + 0.5) * (1.0 / cap)).astype(jnp.int32)
        place = (row - k * cap).astype(F32)
        expert = jnp.bitwise_xor(k, scalar_ref[0])
        before = lax.broadcasted_iota(jnp.int32, (tok_rows, tok_rows), 0)
        after = lax.broadcasted_iota(jnp.int32, (tok_rows, tok_rows), 1)
        earlier = jnp.where(before < after, 1.0, 0.0).astype(BF)
        ready(0, 1)
        named = jnp.zeros((slots, tok_rows), F32)
        gate = jnp.zeros((slots, tok_rows), F32)
        for i in range(top_count):
            hit = ids_ref[i : i + 1, :] == expert
            named = jnp.where(hit, 1.0, named)
            gate = jnp.where(hit, wts_ref[i : i + 1, :], gate)
        rank = mm(named.astype(BF), earlier)
        kept = (named > 0.5) & (rank == place)
        dm = jnp.where(kept, 1.0, 0.0)
        gm = jnp.where(kept, gate, 0.0)
        dmb = dm.astype(BF)
        slot_gate = jnp.sum(gm, axis=1, keepdims=True)
        dm_out[...] = dm
        gm_out[...] = gm
        first = 2 * near_chips * cap
        ready(2)
        x_rows = mm(dmb[first:], tok_ref[...])
        ready(3)
        g_rows = slot_gate[first:] * mm(dmb[first:], cot_ref[...])
        for q in range(far):
            for b in range(2):
                low = (2 * q + b) * cap
                both = jnp.concatenate((x_rows[low : low + cap], g_rows[low : low + cap]), 0)
                if b:
                    core_out[2 * cap * q : 2 * cap * (q + 1), :] = both.astype(BF)
                else:
                    outs[q][...] = both.astype(BF)

    outs = local_call(
        body,
        scalars,
        (ids_t, wts_t, tokens, cotangent),
        [shaped((2 * cap, half))] * far
        + [
            shaped((far * 2 * cap, half)),
            shaped((slots, tok_rows), F32),
            shaped((slots, tok_rows), F32),
            shaped(tokens.shape),
            shaped(cotangent.shape),
        ],
        flops=4 * slots * tok_rows * half,
        staged=4,
        grant=20,
        keep=2,
    )
    return outs[:far], outs[far:]


def gate_tables(scalars, dm, gm, cap, near_chips):
    slots, tok_rows = dm.shape
    near = 2 * near_chips * cap

    def body(_, bufs, outs, ready):
        blank = jnp.zeros((cap, tok_rows), F32)
        for out, low, high in ((outs[0], 0, near), (outs[1], near, slots)):
            gates, picks = [], []
            for k in range(low, high, cap):
                gates += [bufs[1][k : k + cap, :], blank]
                picks += [blank, bufs[0][k : k + cap, :]]
            gate = jnp.transpose(jnp.concatenate(gates, 0))
            one = gate.astype(BF)
            left = gate - one.astype(F32)
            two = left.astype(BF)
            out[0:tok_rows] = one
            out[tok_rows : 2 * tok_rows] = two
            out[2 * tok_rows : 3 * tok_rows] = (left - two.astype(F32)).astype(BF)
            out[3 * tok_rows :] = jnp.transpose(jnp.concatenate(picks, 0)).astype(BF)

    return local_call(
        body,
        scalars,
        (dm, gm),
        (shaped((4 * tok_rows, 2 * near)), shaped((4 * tok_rows, 2 * (slots - near)))),
    )


def near_rows(scalars, dm, gm, tokens, tokens_other, cotangent, cotangent_other, cap, chips):
    tok_rows, half = tokens.shape
    near = 2 * chips * cap

    def body(_, bufs, outs, ready):
        t_own, c_own, dm_ref, gm_ref, t_oth, c_oth = bufs
        dmb = dm_ref[0:near, :].astype(BF)
        slot_gate = jnp.sum(gm_ref[0:near, :], axis=1, keepdims=True)
        for h, (t_ref, c_ref) in enumerate(((t_own, c_own), (t_oth, c_oth))):
            x_rows = mm(dmb, t_ref[...])
            g_rows = slot_gate * mm(dmb, c_ref[...])
            for q in range(chips):
                for b in range(2):
                    low = (2 * q + b) * cap
                    both = jnp.concatenate((x_rows[low : low + cap], g_rows[low : low + cap]), 0)
                    outs[b][q, h] = both.astype(BF)

    return local_call(
        body,
        scalars,
        (tokens, cotangent, dm, gm, tokens_other, cotangent_other),
        [shaped((chips, 2, 2 * cap, half))] * 2,
        flops=8 * near * tok_rows * half,
    )


def ffn(scalar_ref, xs, gs, weight_refs):
    half = xs[0].shape[1]
    gate_w, up_w, down_w = (
        [
            w.at[:, pl.ds(pl.multiple_of(jnp.bitwise_xor(scalar_ref[1], i) * half, half), half)]
            for i in range(2)
        ]
        for w in weight_refs
    )
    gate_pre = mmt(xs[0], gate_w[0][...]) + mmt(xs[1], gate_w[1][...])
    up_pre = mmt(xs[0], up_w[0][...]) + mmt(xs[1], up_w[1][...])
    act, slope = silu_parts(gate_pre)
    hidden = (act * up_pre).astype(BF)
    grad_hidden = mmt(gs[0], down_w[0][...]) + mmt(gs[1], down_w[1][...])
    grad_gate = (grad_hidden * up_pre * slope).astype(BF)
    grad_up = (grad_hidden * act).astype(BF)
    values = [mm(hidden, down_w[i][...]) for i in range(2)]
    inputs = [mm(grad_gate, gate_w[i][...]) + mm(grad_up, up_w[i][...]) for i in range(2)]
    return values, inputs


def ffn_flops(rows, weights):
    return 12 * rows * weights[0].shape[0] * weights[0].shape[1]


def routed_ffn(scalars, near, far, other, weights, cap):
    arrays = list(near) + list(far) + ([other] if far else [])
    count = len(near) + len(far)

    def body(scalar_ref, bufs, outs, ready):
        def views(refs):
            pairs = [(r.at[0], r.at[1]) for r in refs[: len(near)]]
            rest = refs[len(near) :]
            return pairs + [(rest[i], rest[len(far)].at[i]) for i in range(len(far))]

        def pick(h, part):
            segments = []
            for pair in views(bufs[: len(arrays)]):
                block = pair[h][...].astype(F32)
                for b in range(2):
                    low = (2 * b + part) * cap
                    segments.append(block[low : low + cap])
            return jnp.concatenate(segments, 0).astype(BF)

        xs = [pick(0, 0), pick(1, 0)]
        gs = [pick(0, 1), pick(1, 1)]
        values, inputs = ffn(scalar_ref, xs, gs, bufs[len(arrays) :])
        for n, pair in enumerate(views(outs)):
            for h in range(2):
                segments = []
                for b in range(2):
                    low = (2 * n + b) * cap
                    segments += [values[h][low : low + cap], inputs[h][low : low + cap]]
                pair[h][...] = jnp.concatenate(segments, 0).astype(BF)

    outs = local_call(
        body,
        scalars,
        arrays + list(weights),
        [shaped(a.shape) for a in arrays],
        flops=ffn_flops(2 * cap * count, weights),
    )
    return outs if near else (outs[:-1], outs[-1])


def shared_ffn(scalars, tokens, tokens_other, cotangent, cotangent_other, weights):
    tok_rows, half = tokens.shape

    def body(scalar_ref, bufs, outs, ready):
        xs = [bufs[0][...], bufs[2][...]]
        gs = [bufs[1][...], bufs[3][...]]
        values, inputs = ffn(scalar_ref, xs, gs, bufs[4:])
        for h in range(2):
            outs[h][0] = values[h]
            outs[h][1] = inputs[h]

    return local_call(
        body,
        scalars,
        (tokens, cotangent, tokens_other, cotangent_other, *weights),
        [shaped((2, tok_rows, half), F32)] * 2,
        flops=ffn_flops(tok_rows, weights),
    )


def combine(table, blocks):
    tok_rows = table.shape[0] // 4
    sums = mm(table[...], jnp.concatenate(blocks, 0))
    parts = [sums[i * tok_rows : (i + 1) * tok_rows] for i in range(4)]
    return parts[0] + parts[1] + parts[2], parts[3]


def near_combine(scalars, table, own, core0, core, shared_own, shared_other, cap):
    _, tok_rows, half = shared_own.shape
    near = len(own)

    def body(_, bufs, outs, ready):
        table_ref, core0_ref, core_ref, s_own, s_oth = bufs[:5]
        for h, shared in enumerate((s_own, s_oth)):
            blocks = []
            for q in range(near):
                partner = core_ref[q - 1, h, 2 * cap :] if q else core0_ref[h, 2 * cap :]
                blocks += [bufs[5 + q][h, : 2 * cap], partner]
            value, grad = combine(table_ref, blocks)
            outs[h][0] = (shared[0] + value).astype(outs[h].dtype)
            outs[h][1] = (shared[1] + grad).astype(outs[h].dtype)

    return local_call(
        body,
        scalars,
        (table, core0, core, shared_own, shared_other, *own),
        (shaped((2, tok_rows, half), F32), shaped((2, tok_rows, half))),
        flops=64 * tok_rows * near * cap * half,
    )


def far_combine(scalars, table, base, partner, own, core, cap):
    _, tok_rows, half = base.shape
    far = len(own)

    def body(_, bufs, outs, ready):
        table_ref, base_ref, partner_ref = bufs[:3]
        received = bufs[3:]
        blocks = []
        for q in range(far):
            blocks += [received[q][: 2 * cap], received[far + q][2 * cap :]]
        sums = combine(table_ref, blocks)
        for i in range(2):
            outs[i][...] = (base_ref[i] + partner_ref[i].astype(F32) + sums[i]).astype(BF)

    return local_call(
        body,
        scalars,
        (table, base, partner, *own, *core),
        [shaped((tok_rows, half))] * 2,
        flops=32 * tok_rows * far * cap * half,
    )


def paired(*args):
    return paired_steps(*args)


def paired_steps(
    tokens,
    cotangent,
    route_ids,
    route_weights,
    shared_gate,
    shared_up,
    shared_down,
    expert_gate,
    expert_up,
    expert_down,
):
    experts = lax.axis_size("expert")
    tok_rows, top_count = route_ids.shape
    cap = tok_rows * top_count // (2 * experts)
    scalars = jnp.stack([lax.axis_index("expert"), lax.axis_index("tensor")]).astype(jnp.int32)
    routed = (expert_gate[0], expert_up[0], expert_down[0])
    shared = (shared_gate, shared_up, shared_down)

    def across(values):
        return lax.ppermute(values, "tensor", [(0, 1), (1, 0)])

    def exchange(values, k):
        return lax.ppermute(values, "expert", [(i, i ^ k) for i in range(experts)])

    def joined(own, core):
        return jnp.concatenate((own, core), axis=own.ndim - 2)

    chips, near_chips = experts // 2, experts // 4
    own_far, rest = prep(
        scalars, route_ids.T, route_weights.T, tokens, cotangent, experts, cap, near_chips
    )
    core_far, dm, gm, tokens_here, cotangent_here = rest
    tokens_other = across(tokens)
    cotangent_other = across(cotangent)
    core_back = exchange(core_far, 1)
    arrived = {}
    for q in range(near_chips, chips):
        rows = slice((q - near_chips) * 2 * cap, (q - near_chips + 1) * 2 * cap)
        arrived[q] = exchange(joined(own_far[q - near_chips], core_back[rows]), 2 * q)
    near_own, near_out = near_rows(
        scalars, dm, gm, tokens_here, tokens_other, cotangent_here, cotangent_other, cap, near_chips
    )
    near_back = exchange(near_out, 1)
    near_table, far_table = gate_tables(scalars, dm, gm, cap, near_chips)
    near = [joined(near_own[q], near_back[q]) for q in range(near_chips)]
    near = near[:1] + [exchange(near[q], 2 * q) for q in range(1, near_chips)]
    shared_own, shared_other = shared_ffn(
        scalars, tokens_here, tokens_other, cotangent_here, cotangent_other, shared
    )
    out = routed_ffn(scalars, near, (), None, routed, cap)
    home = list(out[:1]) + [exchange(out[q], 2 * q) for q in range(1, near_chips)]
    core0 = exchange(home[0], 1)
    joint = jnp.stack(home[1:])
    core1 = exchange(joint, 1)
    base, partial = near_combine(
        scalars, near_table, home, core0, core1, shared_own, shared_other, cap
    )
    partner = across(partial)
    returned = {}
    for group in FAR_GROUPS:
        rows = [arrived[q] for q in group]
        both = jnp.stack(rows)
        other = across(both)
        own, rest = routed_ffn(scalars, (), rows, other, routed, cap)
        rest = across(rest)
        for n, q in enumerate(group):
            total = (own[n].astype(F32) + rest[n].astype(F32)).astype(BF)
            returned[q] = exchange(total, 2 * q)
    own = [returned[q] for q in range(near_chips, chips)]
    core = [exchange(returned[q], 1) for q in range(near_chips, chips)]
    return far_combine(scalars, far_table, base, partner, own, core, cap)


FAR_GROUPS = ((6,), (7,), (4, 5,))


def serves(mesh_shape, args):
    _, _, route_ids = args[:3]
    experts, tensor = mesh_shape["expert"], mesh_shape["tensor"]
    block, top_count = route_ids.shape[0] // experts, route_ids.shape[1]
    cap = block * top_count // (2 * experts)
    return (
        tensor == 2
        and args[7].shape[0] == experts
        and experts == 16
        and cap % 8 == 0
        and block % 16 == 0
    )


def on_device(
    tokens,
    cotangent,
    route_ids,
    route_weights,
    shared_gate,
    shared_up,
    shared_down,
    expert_gate,
    expert_up,
    expert_down,
):
    expert_count = lax.axis_size("expert")
    tok_rows, top_count = route_ids.shape
    local_experts = expert_gate.shape[0]
    all_experts = local_experts * expert_count
    capacity = tok_rows * top_count // (2 * all_experts)
    slot_total = all_experts * capacity
    flat_ids = route_ids.reshape(-1)
    one_hot = (flat_ids[:, None] == jnp.arange(all_experts, dtype=jnp.int32)[None, :]).astype(
        jnp.int32
    )
    rank_in = jnp.sum((jnp.cumsum(one_hot, axis=0) - one_hot) * one_hot, axis=1)
    kept_mask = rank_in < capacity
    slot_index = jnp.where(kept_mask, flat_ids * capacity + rank_in, slot_total)
    slot_match = jnp.arange(slot_total, dtype=jnp.int32)[:, None] == slot_index[None, :]
    dispatch = jnp.any(slot_match.reshape(slot_total, tok_rows, top_count), axis=2).astype(
        jnp.bfloat16
    )
    gate_flat = route_weights.reshape(-1)
    slot_gate = jnp.sum(jnp.where(slot_match, gate_flat[None, :], 0.0), axis=1)
    gate_dispatch = dispatch.astype(jnp.float32) * slot_gate[:, None]
    x_full, c_full = (
        lax.all_gather(tokens, "tensor", axis=1, tiled=True),
        lax.all_gather(cotangent, "tensor", axis=1, tiled=True),
    )
    x_slots = jnp.dot(dispatch, tokens, preferred_element_type=jnp.float32).astype(jnp.bfloat16)
    g_slots = (
        slot_gate[:, None] * jnp.dot(dispatch, cotangent, preferred_element_type=jnp.float32)
    ).astype(jnp.bfloat16)
    x_part, g_part = (
        lax.all_to_all(x_slots, "expert", split_axis=0, concat_axis=0, tiled=True),
        lax.all_to_all(g_slots, "expert", split_axis=0, concat_axis=0, tiled=True),
    )
    x_recv, g_recv = (
        lax.all_gather(x_part, "tensor", axis=1, tiled=True),
        lax.all_gather(g_part, "tensor", axis=1, tiled=True),
    )

    def owner_layout(values):
        shaped = values.reshape(expert_count, local_experts, capacity, values.shape[-1])
        return shaped.transpose(1, 0, 2, 3).reshape(
            local_experts, expert_count * capacity, values.shape[-1]
        )

    def source_layout(values):
        shaped = values.reshape(local_experts, expert_count, capacity, values.shape[-1])
        return shaped.transpose(1, 0, 2, 3).reshape(slot_total, values.shape[-1])

    x_own = owner_layout(x_recv)
    g_own = owner_layout(g_recv)
    gate_pre = jnp.einsum("erd,efd->erf", x_own, expert_gate, preferred_element_type=jnp.float32)
    up_pre = jnp.einsum("erd,efd->erf", x_own, expert_up, preferred_element_type=jnp.float32)
    act_value, act_slope = silu_parts(gate_pre)
    hidden = (act_value * up_pre).astype(jnp.bfloat16)
    grad_hidden = jnp.einsum("erd,efd->erf", g_own, expert_down, preferred_element_type=jnp.float32)
    grad_gate = (grad_hidden * up_pre * act_slope).astype(jnp.bfloat16)
    grad_up = (grad_hidden * act_value).astype(jnp.bfloat16)
    value_part = source_layout(
        jnp.einsum("erf,efd->erd", hidden, expert_down, preferred_element_type=jnp.float32).astype(
            jnp.bfloat16
        )
    )
    grads_joined = jnp.concatenate((grad_gate, grad_up), axis=2)
    weights_joined = jnp.concatenate((expert_gate, expert_up), axis=1)
    input_term = jnp.einsum(
        "erf,efd->erd", grads_joined, weights_joined, preferred_element_type=jnp.float32
    )
    input_part = source_layout(input_term.astype(jnp.bfloat16))
    shared_gate_pre = jnp.einsum(
        "td,fd->tf", x_full, shared_gate, preferred_element_type=jnp.float32
    )
    shared_up_pre = jnp.einsum("td,fd->tf", x_full, shared_up, preferred_element_type=jnp.float32)
    shared_act, shared_slope = silu_parts(shared_gate_pre)
    shared_hidden = (shared_act * shared_up_pre).astype(jnp.bfloat16)
    shared_value = jnp.dot(shared_hidden, shared_down, preferred_element_type=jnp.float32)
    shared_grad_hidden = jnp.einsum(
        "td,fd->tf", c_full, shared_down, preferred_element_type=jnp.float32
    )
    shared_grad_gate = (shared_grad_hidden * shared_up_pre * shared_slope).astype(jnp.bfloat16)
    shared_grad_up = (shared_grad_hidden * shared_act).astype(jnp.bfloat16)
    shared_input = jnp.dot(shared_grad_gate, shared_gate, preferred_element_type=jnp.float32)
    shared_input = shared_input + jnp.dot(
        shared_grad_up, shared_up, preferred_element_type=jnp.float32
    )
    value_back, input_back = (
        lax.all_to_all(value_part, "expert", split_axis=0, concat_axis=0, tiled=True),
        lax.all_to_all(input_part, "expert", split_axis=0, concat_axis=0, tiled=True),
    )
    early_value = shared_value + jnp.einsum(
        "st,sd->td",
        gate_dispatch,
        value_back.astype(jnp.float32),
        precision=lax.Precision.HIGHEST,
        preferred_element_type=jnp.float32,
    )
    early_input = shared_input + jnp.einsum(
        "st,sd->td",
        dispatch,
        input_back,
        precision=lax.Precision.HIGHEST,
        preferred_element_type=jnp.float32,
    )
    value_total, input_total = (
        lax.psum_scatter(early_value, "tensor", scatter_dimension=1, tiled=True),
        lax.psum_scatter(early_input, "tensor", scatter_dimension=1, tiled=True),
    )
    return (value_total.astype(jnp.bfloat16), input_total.astype(jnp.bfloat16))


def solution(mesh):
    in_specs = (
        P("expert", "tensor"),
        P("expert", "tensor"),
        P("expert", None),
        P("expert", None),
        P("tensor", None),
        P("tensor", None),
        P("tensor", None),
        P("expert", "tensor", None),
        P("expert", "tensor", None),
        P("expert", "tensor", None),
    )
    out_specs = (P("expert", "tensor"), P("expert", "tensor"))

    def layer(*args):
        fits = serves(dict(mesh.shape), args)
        program = jax.shard_map(
            paired if fits else on_device,
            mesh=mesh,
            in_specs=in_specs,
            out_specs=out_specs,
            check_vma=False,
        )
        return program(*args)

    return layer
```

```python
import math

import jax
import jax.numpy as jnp
from jax import lax
from jax.experimental import pallas as pl
from jax.experimental.pallas import tpu as pltpu
from jax.sharding import PartitionSpec as P


WHOLE_OUT = (1, 3,)
WHOLE_BACK = (1, 3,)
GROUPS = ((4,), (5,), (0, 1, 2, 3, 6,), (7,))


BF = jnp.bfloat16
F32 = jnp.float32
ROWS_BY_ROWS = (((1,), (1,)), ((), ()))


def silu_parts(pre_act):
    sigmoid_value = jax.nn.sigmoid(pre_act)
    return (pre_act * sigmoid_value, sigmoid_value * (1.0 + pre_act * (1.0 - sigmoid_value)))


def mm(a, b):
    return jnp.dot(a, b, preferred_element_type=F32)


def mmt(a, b):
    return lax.dot_general(a, b, ROWS_BY_ROWS, preferred_element_type=F32)


def local_call(body, scalars, arrays, outs, flops=0, staged=0, grant=20, keep=0):
    count = len(arrays)

    def kernel(*refs):
        scalar_ref, ins = refs[0], refs[1 : count + 1]
        out_refs = refs[count + 1 : count + 1 + len(outs)]
        sem = refs[-1]
        bufs = list(refs[count + 1 + len(outs) :][: staged - keep])
        bufs += out_refs[len(outs) - keep :] if keep else ()
        copies = [pltpu.make_async_copy(ins[i], bufs[i], sem.at[i]) for i in range(staged)]
        for copy in copies:
            copy.start()

        def ready(*which):
            for i in which:
                copies[i].wait()

        body(scalar_ref, bufs + list(ins[staged:]), out_refs, ready)

    arrays = [
        pltpu.with_memory_space_constraint(a, pltpu.HBM) if i < staged else a
        for i, a in enumerate(arrays)
    ]
    moved = sum(math.prod(a.shape) * a.dtype.itemsize for a in arrays)
    moved += sum(math.prod(o.shape) * o.dtype.itemsize for o in outs)
    whole = pl.BlockSpec(memory_space=pltpu.VMEM)
    return pl.pallas_call(
        kernel,
        out_shape=list(outs),
        in_specs=[pl.BlockSpec(memory_space=pltpu.SMEM)]
        + [pl.BlockSpec(memory_space=pltpu.HBM)] * staged
        + [whole] * (count - staged),
        out_specs=[whole] * len(outs),
        scratch_shapes=[pltpu.VMEM(a.shape, a.dtype) for a in arrays[: staged - keep]]
        + [pltpu.SemaphoreType.DMA((max(staged, 1),))],
        compiler_params=pltpu.CompilerParams(vmem_limit_bytes=grant << 20),
        cost_estimate=pl.CostEstimate(flops=flops, bytes_accessed=moved, transcendentals=0),
    )(scalars, *arrays)


def shaped(shape, dtype=BF):
    return jax.ShapeDtypeStruct(shape, dtype)


def prep(scalars, ids_t, wts_t, tokens, cotangent, experts, cap, chips):
    tok_rows, half = tokens.shape
    top_count = ids_t.shape[0]
    slots = experts * cap
    far = len(chips)

    def body(scalar_ref, bufs, outs, ready):
        ids_ref, wts_ref, tok_ref, cot_ref = bufs
        core_out, dm_out, gm_out = outs[far : far + 3]
        row = lax.broadcasted_iota(jnp.int32, (slots, 1), 0)
        k = ((row.astype(F32) + 0.5) * (1.0 / cap)).astype(jnp.int32)
        place = (row - k * cap).astype(F32)
        expert = jnp.bitwise_xor(k, scalar_ref[0])
        before = lax.broadcasted_iota(jnp.int32, (tok_rows, tok_rows), 0)
        after = lax.broadcasted_iota(jnp.int32, (tok_rows, tok_rows), 1)
        earlier = jnp.where(before < after, 1.0, 0.0).astype(BF)
        ready(0, 1)
        named = jnp.zeros((slots, tok_rows), F32)
        gate = jnp.zeros((slots, tok_rows), F32)
        for i in range(top_count):
            hit = ids_ref[i : i + 1, :] == expert
            named = jnp.where(hit, 1.0, named)
            gate = jnp.where(hit, wts_ref[i : i + 1, :], gate)
        rank = mm(named.astype(BF), earlier)
        kept = (named > 0.5) & (rank == place)
        dm = jnp.where(kept, 1.0, 0.0)
        gm = jnp.where(kept, gate, 0.0)
        dmb = dm.astype(BF)
        slot_gate = jnp.sum(gm, axis=1, keepdims=True)
        dm_out[...] = dm
        gm_out[...] = gm
        first = 2 * min(chips) * cap
        ready(2)
        x_rows = mm(dmb[first:], tok_ref[...])
        ready(3)
        g_rows = slot_gate[first:] * mm(dmb[first:], cot_ref[...])
        for q in range(far):
            for b in range(2):
                low = (2 * chips[q] + b) * cap - first
                both = jnp.concatenate((x_rows[low : low + cap], g_rows[low : low + cap]), 0)
                if b:
                    core_out[2 * cap * q : 2 * cap * (q + 1), :] = both.astype(BF)
                else:
                    outs[q][...] = both.astype(BF)

    outs = local_call(
        body,
        scalars,
        (ids_t, wts_t, tokens, cotangent),
        [shaped((2 * cap, half))] * far
        + [
            shaped((far * 2 * cap, half)),
            shaped((slots, tok_rows), F32),
            shaped((slots, tok_rows), F32),
            shaped(tokens.shape),
            shaped(cotangent.shape),
        ],
        flops=4 * slots * tok_rows * half,
        staged=4,
        grant=20,
        keep=2,
    )
    return outs[:far], outs[far:]


def gate_tables(scalars, dm, gm, cap, near, far):
    _, tok_rows = dm.shape

    def body(_, bufs, outs, ready):
        blank = jnp.zeros((cap, tok_rows), F32)
        for out, chips in zip(outs, (near, far)):
            gates, picks = [], []
            for k in [2 * q + b for q in chips for b in range(2)]:
                rows = slice(k * cap, (k + 1) * cap)
                gates += [bufs[1][rows, :], blank]
                picks += [blank, bufs[0][rows, :]]
            gate = jnp.transpose(jnp.concatenate(gates, 0))
            one = gate.astype(BF)
            left = gate - one.astype(F32)
            two = left.astype(BF)
            out[0:tok_rows] = one
            out[tok_rows : 2 * tok_rows] = two
            out[2 * tok_rows : 3 * tok_rows] = (left - two.astype(F32)).astype(BF)
            out[3 * tok_rows :] = jnp.transpose(jnp.concatenate(picks, 0)).astype(BF)

    return local_call(
        body,
        scalars,
        (dm, gm),
        [shaped((4 * tok_rows, 4 * cap * len(chips))) for chips in (near, far)],
    )


def near_rows(scalars, dm, gm, tokens, tokens_other, cotangent, cotangent_other, cap, chips):
    tok_rows, half = tokens.shape

    def body(_, bufs, outs, ready):
        t_own, c_own, dm_ref, gm_ref, t_oth, c_oth = bufs
        rows = [slice(2 * q * cap, 2 * (q + 1) * cap) for q in chips]
        dmb = jnp.concatenate([dm_ref[r, :] for r in rows], 0).astype(BF)
        gates = jnp.concatenate([gm_ref[r, :] for r in rows], 0)
        slot_gate = jnp.sum(gates, axis=1, keepdims=True)
        for h, (t_ref, c_ref) in enumerate(((t_own, c_own), (t_oth, c_oth))):
            x_rows = mm(dmb, t_ref[...])
            g_rows = slot_gate * mm(dmb, c_ref[...])
            for n in range(len(chips)):
                for b in range(2):
                    low = (2 * n + b) * cap
                    both = jnp.concatenate((x_rows[low : low + cap], g_rows[low : low + cap]), 0)
                    outs[b][n, h] = both.astype(BF)

    return local_call(
        body,
        scalars,
        (tokens, cotangent, dm, gm, tokens_other, cotangent_other),
        [shaped((len(chips), 2, 2 * cap, half))] * 2,
        flops=16 * len(chips) * cap * tok_rows * half,
    )


def ffn(scalar_ref, xs, gs, weight_refs):
    half = xs[0].shape[1]
    gate_w, up_w, down_w = (
        [
            w.at[:, pl.ds(pl.multiple_of(jnp.bitwise_xor(scalar_ref[1], i) * half, half), half)]
            for i in range(2)
        ]
        for w in weight_refs
    )
    gate_pre = mmt(xs[0], gate_w[0][...]) + mmt(xs[1], gate_w[1][...])
    up_pre = mmt(xs[0], up_w[0][...]) + mmt(xs[1], up_w[1][...])
    act, slope = silu_parts(gate_pre)
    hidden = (act * up_pre).astype(BF)
    grad_hidden = mmt(gs[0], down_w[0][...]) + mmt(gs[1], down_w[1][...])
    grad_gate = (grad_hidden * up_pre * slope).astype(BF)
    grad_up = (grad_hidden * act).astype(BF)
    values = [mm(hidden, down_w[i][...]) for i in range(2)]
    inputs = [mm(grad_gate, gate_w[i][...]) + mm(grad_up, up_w[i][...]) for i in range(2)]
    return values, inputs


def ffn_flops(rows, weights):
    return 12 * rows * weights[0].shape[0] * weights[0].shape[1]


def routed_ffn(scalars, ins, other, whole, weights, cap):
    half = weights[0].shape[1] // 2
    extra = [] if other is None else [other]
    arrays = list(ins) + extra
    count = len(ins)
    parted = count - sum(whole)

    def body(scalar_ref, bufs, outs, ready):
        def views(refs, entire):
            pairs, used = [], 0
            for i in range(count):
                if entire[i]:
                    pairs.append((refs[i].at[0], refs[i].at[1]))
                else:
                    pairs.append((refs[i], refs[count].at[used]))
                    used += 1
            return pairs

        given = views(bufs, [len(a.shape) == 3 for a in ins])

        def pick(h, part):
            segments = []
            for pair in given:
                block = pair[h][...].astype(F32)
                for b in range(2):
                    low = (2 * b + part) * cap
                    segments.append(block[low : low + cap])
            return jnp.concatenate(segments, 0).astype(BF)

        xs = [pick(0, 0), pick(1, 0)]
        gs = [pick(0, 1), pick(1, 1)]
        values, inputs = ffn(scalar_ref, xs, gs, bufs[len(arrays) :])
        for n, pair in enumerate(views(outs, whole)):
            for h in range(2):
                segments = []
                for b in range(2):
                    low = (2 * n + b) * cap
                    segments += [values[h][low : low + cap], inputs[h][low : low + cap]]
                pair[h][...] = jnp.concatenate(segments, 0).astype(BF)

    results = [shaped((2, 4 * cap, half)) if w else shaped((4 * cap, half)) for w in whole]
    if parted:
        results.append(shaped((parted, 4 * cap, half)))
    return local_call(
        body, scalars, arrays + list(weights), results, flops=ffn_flops(2 * cap * count, weights)
    )


def shared_ffn(scalars, tokens, tokens_other, cotangent, cotangent_other, weights):
    tok_rows, half = tokens.shape

    def body(scalar_ref, bufs, outs, ready):
        xs = [bufs[0][...], bufs[2][...]]
        gs = [bufs[1][...], bufs[3][...]]
        values, inputs = ffn(scalar_ref, xs, gs, bufs[4:])
        for h in range(2):
            outs[h][0] = values[h]
            outs[h][1] = inputs[h]

    return local_call(
        body,
        scalars,
        (tokens, cotangent, tokens_other, cotangent_other, *weights),
        [shaped((2, tok_rows, half), F32)] * 2,
        flops=ffn_flops(tok_rows, weights),
    )


def combine(table, blocks):
    tok_rows = table.shape[0] // 4
    sums = mm(table[...], jnp.concatenate(blocks, 0))
    parts = [sums[i * tok_rows : (i + 1) * tok_rows] for i in range(4)]
    return parts[0] + parts[1] + parts[2], parts[3]


def near_combine(scalars, table, own, core0, core, shared_own, shared_other, cap):
    _, tok_rows, half = shared_own.shape
    near = len(own)

    def body(_, bufs, outs, ready):
        table_ref, core0_ref, core_ref, s_own, s_oth = bufs[:5]
        for h, shared in enumerate((s_own, s_oth)):
            blocks = []
            for q in range(near):
                partner = core_ref[q - 1, h, 2 * cap :] if q else core0_ref[h, 2 * cap :]
                blocks += [bufs[5 + q][h, : 2 * cap], partner]
            value, grad = combine(table_ref, blocks)
            outs[h][0] = (shared[0] + value).astype(outs[h].dtype)
            outs[h][1] = (shared[1] + grad).astype(outs[h].dtype)

    return local_call(
        body,
        scalars,
        (table, core0, core, shared_own, shared_other, *own),
        (shaped((2, tok_rows, half), F32), shaped((2, tok_rows, half))),
        flops=64 * tok_rows * near * cap * half,
    )


def far_combine(scalars, table, base, partner, own, core, cap):
    _, tok_rows, half = base.shape
    far = len(own)

    def body(_, bufs, outs, ready):
        table_ref, base_ref, partner_ref = bufs[:3]
        received = bufs[3:]
        blocks = []
        for q in range(far):
            blocks += [received[q][: 2 * cap], received[far + q][2 * cap :]]
        sums = combine(table_ref, blocks)
        for i in range(2):
            outs[i][...] = (base_ref[i] + partner_ref[i].astype(F32) + sums[i]).astype(BF)

    return local_call(
        body,
        scalars,
        (table, base, partner, *own, *core),
        [shaped((tok_rows, half))] * 2,
        flops=32 * tok_rows * far * cap * half,
    )


def paired(*args):
    return paired_steps(*args)


def paired_steps(
    tokens,
    cotangent,
    route_ids,
    route_weights,
    shared_gate,
    shared_up,
    shared_down,
    expert_gate,
    expert_up,
    expert_down,
):
    experts = lax.axis_size("expert")
    tok_rows, top_count = route_ids.shape
    cap = tok_rows * top_count // (2 * experts)
    scalars = jnp.stack([lax.axis_index("expert"), lax.axis_index("tensor")]).astype(jnp.int32)
    routed = (expert_gate[0], expert_up[0], expert_down[0])
    shared = (shared_gate, shared_up, shared_down)

    def across(values):
        return lax.ppermute(values, "tensor", [(0, 1), (1, 0)])

    def exchange(values, k):
        return lax.ppermute(values, "expert", [(i, i ^ k) for i in range(experts)])

    def joined(own, core):
        return jnp.concatenate((own, core), axis=own.ndim - 2)

    chips = range(1, experts // 2)
    out_halves = [q for q in chips if q not in WHOLE_OUT]
    back_halves = [q for q in chips if q not in WHOLE_BACK]
    own_far, rest = prep(
        scalars, route_ids.T, route_weights.T, tokens, cotangent, experts, cap, out_halves
    )
    core_far, dm, gm, tokens_here, cotangent_here = rest
    tokens_other = across(tokens)
    cotangent_other = across(cotangent)
    core_back = exchange(core_far, 1)
    arrived = {}
    for n, q in enumerate(out_halves):
        rows = joined(own_far[n], core_back[2 * cap * n : 2 * cap * (n + 1)])
        arrived[q] = exchange(rows, 2 * q)
    near = (0, *WHOLE_OUT)
    near_own, near_out = near_rows(
        scalars, dm, gm, tokens_here, tokens_other, cotangent_here, cotangent_other, cap, near
    )
    near_back = exchange(near_out, 1)
    for n, q in enumerate(near):
        rows = joined(near_own[n], near_back[n])
        arrived[q] = exchange(rows, 2 * q) if q else rows
    near_table, far_table = gate_tables(scalars, dm, gm, cap, (0, *WHOLE_BACK), back_halves)
    shared_own, shared_other = shared_ffn(
        scalars, tokens_here, tokens_other, cotangent_here, cotangent_other, shared
    )
    home = {}
    for group in GROUPS:
        halves = [arrived[q] for q in group if q in out_halves]
        other = None
        if halves:
            other = jnp.stack(halves)
            other = across(other)
        whole = [q not in back_halves for q in group]
        ins = [arrived[q] for q in group]
        results = routed_ffn(scalars, ins, other, whole, routed, cap)
        rest = across(results[-1]) if not all(whole) else None
        used = 0
        for q, entire, result in zip(group, whole, results):
            if entire:
                home[q] = exchange(result, 2 * q) if q else result
            else:
                total = (result.astype(F32) + rest[used].astype(F32)).astype(BF)
                home[q] = exchange(total, 2 * q)
                used += 1
    core0 = exchange(home[0], 1)
    joint = jnp.stack([home[q] for q in WHOLE_BACK])
    core1 = exchange(joint, 1)
    near_home = [home[q] for q in (0, *WHOLE_BACK)]
    base, partial = near_combine(
        scalars, near_table, near_home, core0, core1, shared_own, shared_other, cap
    )
    partner = across(partial)
    own = [home[q] for q in back_halves]
    core = [exchange(home[q], 1) for q in back_halves]
    return far_combine(scalars, far_table, base, partner, own, core, cap)


def serves(mesh_shape, args):
    _, _, route_ids = args[:3]
    experts, tensor = mesh_shape["expert"], mesh_shape["tensor"]
    block, top_count = route_ids.shape[0] // experts, route_ids.shape[1]
    cap = block * top_count // (2 * experts)
    return (
        tensor == 2
        and args[7].shape[0] == experts
        and experts == 16
        and cap % 8 == 0
        and block % 16 == 0
    )


def on_device(
    tokens,
    cotangent,
    route_ids,
    route_weights,
    shared_gate,
    shared_up,
    shared_down,
    expert_gate,
    expert_up,
    expert_down,
):
    expert_count = lax.axis_size("expert")
    tok_rows, top_count = route_ids.shape
    local_experts = expert_gate.shape[0]
    all_experts = local_experts * expert_count
    capacity = tok_rows * top_count // (2 * all_experts)
    slot_total = all_experts * capacity
    flat_ids = route_ids.reshape(-1)
    one_hot = (flat_ids[:, None] == jnp.arange(all_experts, dtype=jnp.int32)[None, :]).astype(
        jnp.int32
    )
    rank_in = jnp.sum((jnp.cumsum(one_hot, axis=0) - one_hot) * one_hot, axis=1)
    kept_mask = rank_in < capacity
    slot_index = jnp.where(kept_mask, flat_ids * capacity + rank_in, slot_total)
    slot_match = jnp.arange(slot_total, dtype=jnp.int32)[:, None] == slot_index[None, :]
    dispatch = jnp.any(slot_match.reshape(slot_total, tok_rows, top_count), axis=2).astype(
        jnp.bfloat16
    )
    gate_flat = route_weights.reshape(-1)
    slot_gate = jnp.sum(jnp.where(slot_match, gate_flat[None, :], 0.0), axis=1)
    gate_dispatch = dispatch.astype(jnp.float32) * slot_gate[:, None]
    x_full, c_full = (
        lax.all_gather(tokens, "tensor", axis=1, tiled=True),
        lax.all_gather(cotangent, "tensor", axis=1, tiled=True),
    )
    x_slots = jnp.dot(dispatch, tokens, preferred_element_type=jnp.float32).astype(jnp.bfloat16)
    g_slots = (
        slot_gate[:, None] * jnp.dot(dispatch, cotangent, preferred_element_type=jnp.float32)
    ).astype(jnp.bfloat16)
    x_part, g_part = (
        lax.all_to_all(x_slots, "expert", split_axis=0, concat_axis=0, tiled=True),
        lax.all_to_all(g_slots, "expert", split_axis=0, concat_axis=0, tiled=True),
    )
    x_recv, g_recv = (
        lax.all_gather(x_part, "tensor", axis=1, tiled=True),
        lax.all_gather(g_part, "tensor", axis=1, tiled=True),
    )

    def owner_layout(values):
        shaped = values.reshape(expert_count, local_experts, capacity, values.shape[-1])
        return shaped.transpose(1, 0, 2, 3).reshape(
            local_experts, expert_count * capacity, values.shape[-1]
        )

    def source_layout(values):
        shaped = values.reshape(local_experts, expert_count, capacity, values.shape[-1])
        return shaped.transpose(1, 0, 2, 3).reshape(slot_total, values.shape[-1])

    x_own = owner_layout(x_recv)
    g_own = owner_layout(g_recv)
    gate_pre = jnp.einsum("erd,efd->erf", x_own, expert_gate, preferred_element_type=jnp.float32)
    up_pre = jnp.einsum("erd,efd->erf", x_own, expert_up, preferred_element_type=jnp.float32)
    act_value, act_slope = silu_parts(gate_pre)
    hidden = (act_value * up_pre).astype(jnp.bfloat16)
    grad_hidden = jnp.einsum("erd,efd->erf", g_own, expert_down, preferred_element_type=jnp.float32)
    grad_gate = (grad_hidden * up_pre * act_slope).astype(jnp.bfloat16)
    grad_up = (grad_hidden * act_value).astype(jnp.bfloat16)
    value_part = source_layout(
        jnp.einsum("erf,efd->erd", hidden, expert_down, preferred_element_type=jnp.float32).astype(
            jnp.bfloat16
        )
    )
    grads_joined = jnp.concatenate((grad_gate, grad_up), axis=2)
    weights_joined = jnp.concatenate((expert_gate, expert_up), axis=1)
    input_term = jnp.einsum(
        "erf,efd->erd", grads_joined, weights_joined, preferred_element_type=jnp.float32
    )
    input_part = source_layout(input_term.astype(jnp.bfloat16))
    shared_gate_pre = jnp.einsum(
        "td,fd->tf", x_full, shared_gate, preferred_element_type=jnp.float32
    )
    shared_up_pre = jnp.einsum("td,fd->tf", x_full, shared_up, preferred_element_type=jnp.float32)
    shared_act, shared_slope = silu_parts(shared_gate_pre)
    shared_hidden = (shared_act * shared_up_pre).astype(jnp.bfloat16)
    shared_value = jnp.dot(shared_hidden, shared_down, preferred_element_type=jnp.float32)
    shared_grad_hidden = jnp.einsum(
        "td,fd->tf", c_full, shared_down, preferred_element_type=jnp.float32
    )
    shared_grad_gate = (shared_grad_hidden * shared_up_pre * shared_slope).astype(jnp.bfloat16)
    shared_grad_up = (shared_grad_hidden * shared_act).astype(jnp.bfloat16)
    shared_input = jnp.dot(shared_grad_gate, shared_gate, preferred_element_type=jnp.float32)
    shared_input = shared_input + jnp.dot(
        shared_grad_up, shared_up, preferred_element_type=jnp.float32
    )
    value_back, input_back = (
        lax.all_to_all(value_part, "expert", split_axis=0, concat_axis=0, tiled=True),
        lax.all_to_all(input_part, "expert", split_axis=0, concat_axis=0, tiled=True),
    )
    early_value = shared_value + jnp.einsum(
        "st,sd->td",
        gate_dispatch,
        value_back.astype(jnp.float32),
        precision=lax.Precision.HIGHEST,
        preferred_element_type=jnp.float32,
    )
    early_input = shared_input + jnp.einsum(
        "st,sd->td",
        dispatch,
        input_back,
        precision=lax.Precision.HIGHEST,
        preferred_element_type=jnp.float32,
    )
    value_total, input_total = (
        lax.psum_scatter(early_value, "tensor", scatter_dimension=1, tiled=True),
        lax.psum_scatter(early_input, "tensor", scatter_dimension=1, tiled=True),
    )
    return (value_total.astype(jnp.bfloat16), input_total.astype(jnp.bfloat16))


def solution(mesh):
    in_specs = (
        P("expert", "tensor"),
        P("expert", "tensor"),
        P("expert", None),
        P("expert", None),
        P("tensor", None),
        P("tensor", None),
        P("tensor", None),
        P("expert", "tensor", None),
        P("expert", "tensor", None),
        P("expert", "tensor", None),
    )
    out_specs = (P("expert", "tensor"), P("expert", "tensor"))

    def layer(*args):
        fits = serves(dict(mesh.shape), args)
        program = jax.shard_map(
            paired if fits else on_device,
            mesh=mesh,
            in_specs=in_specs,
            out_specs=out_specs,
            check_vma=False,
        )
        return program(*args)

    return layer
```

```python
import math

import jax
import jax.numpy as jnp
from jax import lax
from jax.experimental import pallas as pl
from jax.experimental.pallas import tpu as pltpu
from jax.sharding import PartitionSpec as P


WHOLE_OUT = (1, 2,)
WHOLE_BACK = (1, 3,)
GROUPS = ((4,), (2, 5,), (0, 1, 3, 6,), (7,))


BF = jnp.bfloat16
F32 = jnp.float32
ROWS_BY_ROWS = (((1,), (1,)), ((), ()))


def silu_parts(pre_act):
    sigmoid_value = jax.nn.sigmoid(pre_act)
    return (pre_act * sigmoid_value, sigmoid_value * (1.0 + pre_act * (1.0 - sigmoid_value)))


def mm(a, b):
    return jnp.dot(a, b, preferred_element_type=F32)


def mmt(a, b):
    return lax.dot_general(a, b, ROWS_BY_ROWS, preferred_element_type=F32)


def local_call(body, scalars, arrays, outs, flops=0, staged=0, grant=20, keep=0):
    count = len(arrays)

    def kernel(*refs):
        scalar_ref, ins = refs[0], refs[1 : count + 1]
        out_refs = refs[count + 1 : count + 1 + len(outs)]
        sem = refs[-1]
        bufs = list(refs[count + 1 + len(outs) :][: staged - keep])
        bufs += out_refs[len(outs) - keep :] if keep else ()
        copies = [pltpu.make_async_copy(ins[i], bufs[i], sem.at[i]) for i in range(staged)]
        for copy in copies:
            copy.start()

        def ready(*which):
            for i in which:
                copies[i].wait()

        body(scalar_ref, bufs + list(ins[staged:]), out_refs, ready)

    arrays = [
        pltpu.with_memory_space_constraint(a, pltpu.HBM) if i < staged else a
        for i, a in enumerate(arrays)
    ]
    moved = sum(math.prod(a.shape) * a.dtype.itemsize for a in arrays)
    moved += sum(math.prod(o.shape) * o.dtype.itemsize for o in outs)
    whole = pl.BlockSpec(memory_space=pltpu.VMEM)
    return pl.pallas_call(
        kernel,
        out_shape=list(outs),
        in_specs=[pl.BlockSpec(memory_space=pltpu.SMEM)]
        + [pl.BlockSpec(memory_space=pltpu.HBM)] * staged
        + [whole] * (count - staged),
        out_specs=[whole] * len(outs),
        scratch_shapes=[pltpu.VMEM(a.shape, a.dtype) for a in arrays[: staged - keep]]
        + [pltpu.SemaphoreType.DMA((max(staged, 1),))],
        compiler_params=pltpu.CompilerParams(vmem_limit_bytes=grant << 20),
        cost_estimate=pl.CostEstimate(flops=flops, bytes_accessed=moved, transcendentals=0),
    )(scalars, *arrays)


def shaped(shape, dtype=BF):
    return jax.ShapeDtypeStruct(shape, dtype)


def prep(scalars, ids_t, wts_t, tokens, cotangent, experts, cap, chips):
    tok_rows, half = tokens.shape
    top_count = ids_t.shape[0]
    slots = experts * cap
    far = len(chips)

    def body(scalar_ref, bufs, outs, ready):
        ids_ref, wts_ref, tok_ref, cot_ref = bufs
        core_out, dm_out, gm_out = outs[far : far + 3]
        row = lax.broadcasted_iota(jnp.int32, (slots, 1), 0)
        k = ((row.astype(F32) + 0.5) * (1.0 / cap)).astype(jnp.int32)
        place = (row - k * cap).astype(F32)
        expert = jnp.bitwise_xor(k, scalar_ref[0])
        before = lax.broadcasted_iota(jnp.int32, (tok_rows, tok_rows), 0)
        after = lax.broadcasted_iota(jnp.int32, (tok_rows, tok_rows), 1)
        earlier = jnp.where(before < after, 1.0, 0.0).astype(BF)
        ready(0, 1)
        named = jnp.zeros((slots, tok_rows), F32)
        gate = jnp.zeros((slots, tok_rows), F32)
        for i in range(top_count):
            hit = ids_ref[i : i + 1, :] == expert
            named = jnp.where(hit, 1.0, named)
            gate = jnp.where(hit, wts_ref[i : i + 1, :], gate)
        rank = mm(named.astype(BF), earlier)
        kept = (named > 0.5) & (rank == place)
        dm = jnp.where(kept, 1.0, 0.0)
        gm = jnp.where(kept, gate, 0.0)
        dmb = dm.astype(BF)
        slot_gate = jnp.sum(gm, axis=1, keepdims=True)
        dm_out[...] = dm
        gm_out[...] = gm
        first = 2 * min(chips) * cap
        ready(2)
        x_rows = mm(dmb[first:], tok_ref[...])
        ready(3)
        g_rows = slot_gate[first:] * mm(dmb[first:], cot_ref[...])
        for q in range(far):
            for b in range(2):
                low = (2 * chips[q] + b) * cap - first
                both = jnp.concatenate((x_rows[low : low + cap], g_rows[low : low + cap]), 0)
                if b:
                    core_out[2 * cap * q : 2 * cap * (q + 1), :] = both.astype(BF)
                else:
                    outs[q][...] = both.astype(BF)

    outs = local_call(
        body,
        scalars,
        (ids_t, wts_t, tokens, cotangent),
        [shaped((2 * cap, half))] * far
        + [
            shaped((far * 2 * cap, half)),
            shaped((slots, tok_rows), F32),
            shaped((slots, tok_rows), F32),
            shaped(tokens.shape),
            shaped(cotangent.shape),
        ],
        flops=4 * slots * tok_rows * half,
        staged=4,
        grant=20,
        keep=2,
    )
    return outs[:far], outs[far:]


def gate_tables(scalars, dm, gm, cap, near, far):
    _, tok_rows = dm.shape

    def body(_, bufs, outs, ready):
        blank = jnp.zeros((cap, tok_rows), F32)
        for out, chips in zip(outs, (near, far)):
            gates, picks = [], []
            for k in [2 * q + b for q in chips for b in range(2)]:
                rows = slice(k * cap, (k + 1) * cap)
                gates += [bufs[1][rows, :], blank]
                picks += [blank, bufs[0][rows, :]]
            gate = jnp.transpose(jnp.concatenate(gates, 0))
            one = gate.astype(BF)
            left = gate - one.astype(F32)
            two = left.astype(BF)
            out[0:tok_rows] = one
            out[tok_rows : 2 * tok_rows] = two
            out[2 * tok_rows : 3 * tok_rows] = (left - two.astype(F32)).astype(BF)
            out[3 * tok_rows :] = jnp.transpose(jnp.concatenate(picks, 0)).astype(BF)

    return local_call(
        body,
        scalars,
        (dm, gm),
        [shaped((4 * tok_rows, 4 * cap * len(chips))) for chips in (near, far)],
    )


def near_rows(scalars, dm, gm, tokens, tokens_other, cotangent, cotangent_other, cap, chips):
    tok_rows, half = tokens.shape

    def body(_, bufs, outs, ready):
        t_own, c_own, dm_ref, gm_ref, t_oth, c_oth = bufs
        rows = [slice(2 * q * cap, 2 * (q + 1) * cap) for q in chips]
        dmb = jnp.concatenate([dm_ref[r, :] for r in rows], 0).astype(BF)
        gates = jnp.concatenate([gm_ref[r, :] for r in rows], 0)
        slot_gate = jnp.sum(gates, axis=1, keepdims=True)
        for h, (t_ref, c_ref) in enumerate(((t_own, c_own), (t_oth, c_oth))):
            x_rows = mm(dmb, t_ref[...])
            g_rows = slot_gate * mm(dmb, c_ref[...])
            for n in range(len(chips)):
                for b in range(2):
                    low = (2 * n + b) * cap
                    both = jnp.concatenate((x_rows[low : low + cap], g_rows[low : low + cap]), 0)
                    outs[b][n, h] = both.astype(BF)

    return local_call(
        body,
        scalars,
        (tokens, cotangent, dm, gm, tokens_other, cotangent_other),
        [shaped((len(chips), 2, 2 * cap, half))] * 2,
        flops=16 * len(chips) * cap * tok_rows * half,
    )


def transposed(scalars, weights):
    def body(_, bufs, outs, ready):
        for i in range(len(weights)):
            ready(i)
            outs[i][...] = jnp.transpose(bufs[i][...])

    return local_call(
        body, scalars, weights, [shaped(w.shape[::-1]) for w in weights], staged=len(weights)
    )


def ffn(scalar_ref, xs, gs, weight_refs):
    half = xs[0].shape[1]
    parts = [
        pl.ds(pl.multiple_of(jnp.bitwise_xor(scalar_ref[1], i) * half, half), half)
        for i in range(2)
    ]
    gate_w, up_w, down_w = ([w.at[:, part] for part in parts] for w in weight_refs[:3])

    def over_features(rows, w):
        if len(weight_refs) > 3:
            return sum(mm(rows[i], weight_refs[3 + w][parts[i], :]) for i in range(2))
        return sum(mmt(rows[i], weight_refs[w][:, parts[i]]) for i in range(2))

    gate_pre = over_features(xs, 0)
    up_pre = over_features(xs, 1)
    act, slope = silu_parts(gate_pre)
    hidden = (act * up_pre).astype(BF)
    grad_hidden = over_features(gs, 2)
    grad_gate = (grad_hidden * up_pre * slope).astype(BF)
    grad_up = (grad_hidden * act).astype(BF)
    values = [mm(hidden, down_w[i][...]) for i in range(2)]
    inputs = [mm(grad_gate, gate_w[i][...]) + mm(grad_up, up_w[i][...]) for i in range(2)]
    return values, inputs


def ffn_flops(rows, weights):
    return 12 * rows * weights[0].shape[0] * weights[0].shape[1]


def routed_ffn(scalars, ins, other, whole, weights, cap):
    half = weights[0].shape[1] // 2
    extra = [] if other is None else [other]
    arrays = list(ins) + extra
    count = len(ins)
    parted = count - sum(whole)

    def body(scalar_ref, bufs, outs, ready):
        def views(refs, entire):
            pairs, used = [], 0
            for i in range(count):
                if entire[i]:
                    pairs.append((refs[i].at[0], refs[i].at[1]))
                else:
                    pairs.append((refs[i], refs[count].at[used]))
                    used += 1
            return pairs

        given = views(bufs, [len(a.shape) == 3 for a in ins])

        def pick(h, part):
            segments = []
            for pair in given:
                block = pair[h][...].astype(F32)
                for b in range(2):
                    low = (2 * b + part) * cap
                    segments.append(block[low : low + cap])
            return jnp.concatenate(segments, 0).astype(BF)

        xs = [pick(0, 0), pick(1, 0)]
        gs = [pick(0, 1), pick(1, 1)]
        values, inputs = ffn(scalar_ref, xs, gs, bufs[len(arrays) :])
        for n, pair in enumerate(views(outs, whole)):
            for h in range(2):
                segments = []
                for b in range(2):
                    low = (2 * n + b) * cap
                    segments += [values[h][low : low + cap], inputs[h][low : low + cap]]
                pair[h][...] = jnp.concatenate(segments, 0).astype(BF)

    results = [shaped((2, 4 * cap, half)) if w else shaped((4 * cap, half)) for w in whole]
    if parted:
        results.append(shaped((parted, 4 * cap, half)))
    return local_call(
        body, scalars, arrays + list(weights), results, flops=ffn_flops(2 * cap * count, weights)
    )


def shared_ffn(scalars, tokens, tokens_other, cotangent, cotangent_other, weights):
    tok_rows, half = tokens.shape

    def body(scalar_ref, bufs, outs, ready):
        xs = [bufs[0][...], bufs[2][...]]
        gs = [bufs[1][...], bufs[3][...]]
        values, inputs = ffn(scalar_ref, xs, gs, bufs[4:])
        for h in range(2):
            outs[h][0] = values[h]
            outs[h][1] = inputs[h]

    return local_call(
        body,
        scalars,
        (tokens, cotangent, tokens_other, cotangent_other, *weights),
        [shaped((2, tok_rows, half), F32)] * 2,
        flops=ffn_flops(tok_rows, weights),
    )


def combine(table, blocks):
    tok_rows = table.shape[0] // 4
    sums = mm(table[...], jnp.concatenate(blocks, 0))
    parts = [sums[i * tok_rows : (i + 1) * tok_rows] for i in range(4)]
    return parts[0] + parts[1] + parts[2], parts[3]


def near_combine(scalars, table, own, core0, core, shared_own, shared_other, cap):
    _, tok_rows, half = shared_own.shape
    near = len(own)

    def body(_, bufs, outs, ready):
        table_ref, core0_ref, core_ref, s_own, s_oth = bufs[:5]
        for h, shared in enumerate((s_own, s_oth)):
            blocks = []
            for q in range(near):
                partner = core_ref[q - 1, h, 2 * cap :] if q else core0_ref[h, 2 * cap :]
                blocks += [bufs[5 + q][h, : 2 * cap], partner]
            value, grad = combine(table_ref, blocks)
            outs[h][0] = (shared[0] + value).astype(outs[h].dtype)
            outs[h][1] = (shared[1] + grad).astype(outs[h].dtype)

    return local_call(
        body,
        scalars,
        (table, core0, core, shared_own, shared_other, *own),
        (shaped((2, tok_rows, half), F32), shaped((2, tok_rows, half))),
        flops=64 * tok_rows * near * cap * half,
    )


def far_combine(scalars, table, base, partner, own, core, cap):
    _, tok_rows, half = base.shape
    far = len(own)

    def body(_, bufs, outs, ready):
        table_ref, base_ref, partner_ref = bufs[:3]
        received = bufs[3:]
        blocks = []
        for q in range(far):
            blocks += [received[q][: 2 * cap], received[far + q][2 * cap :]]
        sums = combine(table_ref, blocks)
        for i in range(2):
            outs[i][...] = (base_ref[i] + partner_ref[i].astype(F32) + sums[i]).astype(BF)

    return local_call(
        body,
        scalars,
        (table, base, partner, *own, *core),
        [shaped((tok_rows, half))] * 2,
        flops=32 * tok_rows * far * cap * half,
    )


def paired(*args):
    return paired_steps(*args)


def paired_steps(
    tokens,
    cotangent,
    route_ids,
    route_weights,
    shared_gate,
    shared_up,
    shared_down,
    expert_gate,
    expert_up,
    expert_down,
):
    experts = lax.axis_size("expert")
    tok_rows, top_count = route_ids.shape
    cap = tok_rows * top_count // (2 * experts)
    scalars = jnp.stack([lax.axis_index("expert"), lax.axis_index("tensor")]).astype(jnp.int32)
    routed = (expert_gate[0], expert_up[0], expert_down[0])
    shared = (shared_gate, shared_up, shared_down)

    def across(values):
        return lax.ppermute(values, "tensor", [(0, 1), (1, 0)])

    def exchange(values, k):
        return lax.ppermute(values, "expert", [(i, i ^ k) for i in range(experts)])

    def joined(own, core):
        return jnp.concatenate((own, core), axis=own.ndim - 2)

    chips = range(1, experts // 2)
    out_halves = [q for q in chips if q not in WHOLE_OUT]
    back_halves = [q for q in chips if q not in WHOLE_BACK]
    own_far, rest = prep(
        scalars, route_ids.T, route_weights.T, tokens, cotangent, experts, cap, out_halves
    )
    core_far, dm, gm, tokens_here, cotangent_here = rest
    tokens_other = across(tokens)
    cotangent_other = across(cotangent)
    core_back = exchange(core_far, 1)
    arrived = {}
    for n, q in enumerate(out_halves):
        rows = joined(own_far[n], core_back[2 * cap * n : 2 * cap * (n + 1)])
        arrived[q] = exchange(rows, 2 * q)
    near = (0, *WHOLE_OUT)
    near_own, near_out = near_rows(
        scalars, dm, gm, tokens_here, tokens_other, cotangent_here, cotangent_other, cap, near
    )
    near_back = exchange(near_out, 1)
    for n, q in enumerate(near):
        rows = joined(near_own[n], near_back[n])
        arrived[q] = exchange(rows, 2 * q) if q else rows
    near_table, far_table = gate_tables(scalars, dm, gm, cap, (0, *WHOLE_BACK), back_halves)
    shared_own, shared_other = shared_ffn(
        scalars, tokens_here, tokens_other, cotangent_here, cotangent_other, shared
    )
    routed_both = (*routed, *transposed(scalars, routed))
    home = {}
    for group in GROUPS:
        halves = [arrived[q] for q in group if q in out_halves]
        other = None
        if halves:
            other = jnp.stack(halves)
            other = across(other)
        whole = [q not in back_halves for q in group]
        ins = [arrived[q] for q in group]
        results = routed_ffn(scalars, ins, other, whole, routed_both, cap)
        rest = across(results[-1]) if not all(whole) else None
        used = 0
        for q, entire, result in zip(group, whole, results):
            if entire:
                home[q] = exchange(result, 2 * q) if q else result
            else:
                total = (result.astype(F32) + rest[used].astype(F32)).astype(BF)
                home[q] = exchange(total, 2 * q)
                used += 1
    core0 = exchange(home[0], 1)
    joint = jnp.stack([home[q] for q in WHOLE_BACK])
    core1 = exchange(joint, 1)
    near_home = [home[q] for q in (0, *WHOLE_BACK)]
    base, partial = near_combine(
        scalars, near_table, near_home, core0, core1, shared_own, shared_other, cap
    )
    partner = across(partial)
    own = [home[q] for q in back_halves]
    core = [exchange(home[q], 1) for q in back_halves]
    return far_combine(scalars, far_table, base, partner, own, core, cap)


def serves(mesh_shape, args):
    _, _, route_ids = args[:3]
    experts, tensor = mesh_shape["expert"], mesh_shape["tensor"]
    block, top_count = route_ids.shape[0] // experts, route_ids.shape[1]
    cap = block * top_count // (2 * experts)
    return (
        tensor == 2
        and args[7].shape[0] == experts
        and experts == 16
        and cap % 8 == 0
        and block % 16 == 0
    )


def on_device(
    tokens,
    cotangent,
    route_ids,
    route_weights,
    shared_gate,
    shared_up,
    shared_down,
    expert_gate,
    expert_up,
    expert_down,
):
    expert_count = lax.axis_size("expert")
    tok_rows, top_count = route_ids.shape
    local_experts = expert_gate.shape[0]
    all_experts = local_experts * expert_count
    capacity = tok_rows * top_count // (2 * all_experts)
    slot_total = all_experts * capacity
    flat_ids = route_ids.reshape(-1)
    one_hot = (flat_ids[:, None] == jnp.arange(all_experts, dtype=jnp.int32)[None, :]).astype(
        jnp.int32
    )
    rank_in = jnp.sum((jnp.cumsum(one_hot, axis=0) - one_hot) * one_hot, axis=1)
    kept_mask = rank_in < capacity
    slot_index = jnp.where(kept_mask, flat_ids * capacity + rank_in, slot_total)
    slot_match = jnp.arange(slot_total, dtype=jnp.int32)[:, None] == slot_index[None, :]
    dispatch = jnp.any(slot_match.reshape(slot_total, tok_rows, top_count), axis=2).astype(
        jnp.bfloat16
    )
    gate_flat = route_weights.reshape(-1)
    slot_gate = jnp.sum(jnp.where(slot_match, gate_flat[None, :], 0.0), axis=1)
    gate_dispatch = dispatch.astype(jnp.float32) * slot_gate[:, None]
    x_full, c_full = (
        lax.all_gather(tokens, "tensor", axis=1, tiled=True),
        lax.all_gather(cotangent, "tensor", axis=1, tiled=True),
    )
    x_slots = jnp.dot(dispatch, tokens, preferred_element_type=jnp.float32).astype(jnp.bfloat16)
    g_slots = (
        slot_gate[:, None] * jnp.dot(dispatch, cotangent, preferred_element_type=jnp.float32)
    ).astype(jnp.bfloat16)
    x_part, g_part = (
        lax.all_to_all(x_slots, "expert", split_axis=0, concat_axis=0, tiled=True),
        lax.all_to_all(g_slots, "expert", split_axis=0, concat_axis=0, tiled=True),
    )
    x_recv, g_recv = (
        lax.all_gather(x_part, "tensor", axis=1, tiled=True),
        lax.all_gather(g_part, "tensor", axis=1, tiled=True),
    )

    def owner_layout(values):
        shaped = values.reshape(expert_count, local_experts, capacity, values.shape[-1])
        return shaped.transpose(1, 0, 2, 3).reshape(
            local_experts, expert_count * capacity, values.shape[-1]
        )

    def source_layout(values):
        shaped = values.reshape(local_experts, expert_count, capacity, values.shape[-1])
        return shaped.transpose(1, 0, 2, 3).reshape(slot_total, values.shape[-1])

    x_own = owner_layout(x_recv)
    g_own = owner_layout(g_recv)
    gate_pre = jnp.einsum("erd,efd->erf", x_own, expert_gate, preferred_element_type=jnp.float32)
    up_pre = jnp.einsum("erd,efd->erf", x_own, expert_up, preferred_element_type=jnp.float32)
    act_value, act_slope = silu_parts(gate_pre)
    hidden = (act_value * up_pre).astype(jnp.bfloat16)
    grad_hidden = jnp.einsum("erd,efd->erf", g_own, expert_down, preferred_element_type=jnp.float32)
    grad_gate = (grad_hidden * up_pre * act_slope).astype(jnp.bfloat16)
    grad_up = (grad_hidden * act_value).astype(jnp.bfloat16)
    value_part = source_layout(
        jnp.einsum("erf,efd->erd", hidden, expert_down, preferred_element_type=jnp.float32).astype(
            jnp.bfloat16
        )
    )
    grads_joined = jnp.concatenate((grad_gate, grad_up), axis=2)
    weights_joined = jnp.concatenate((expert_gate, expert_up), axis=1)
    input_term = jnp.einsum(
        "erf,efd->erd", grads_joined, weights_joined, preferred_element_type=jnp.float32
    )
    input_part = source_layout(input_term.astype(jnp.bfloat16))
    shared_gate_pre = jnp.einsum(
        "td,fd->tf", x_full, shared_gate, preferred_element_type=jnp.float32
    )
    shared_up_pre = jnp.einsum("td,fd->tf", x_full, shared_up, preferred_element_type=jnp.float32)
    shared_act, shared_slope = silu_parts(shared_gate_pre)
    shared_hidden = (shared_act * shared_up_pre).astype(jnp.bfloat16)
    shared_value = jnp.dot(shared_hidden, shared_down, preferred_element_type=jnp.float32)
    shared_grad_hidden = jnp.einsum(
        "td,fd->tf", c_full, shared_down, preferred_element_type=jnp.float32
    )
    shared_grad_gate = (shared_grad_hidden * shared_up_pre * shared_slope).astype(jnp.bfloat16)
    shared_grad_up = (shared_grad_hidden * shared_act).astype(jnp.bfloat16)
    shared_input = jnp.dot(shared_grad_gate, shared_gate, preferred_element_type=jnp.float32)
    shared_input = shared_input + jnp.dot(
        shared_grad_up, shared_up, preferred_element_type=jnp.float32
    )
    value_back, input_back = (
        lax.all_to_all(value_part, "expert", split_axis=0, concat_axis=0, tiled=True),
        lax.all_to_all(input_part, "expert", split_axis=0, concat_axis=0, tiled=True),
    )
    early_value = shared_value + jnp.einsum(
        "st,sd->td",
        gate_dispatch,
        value_back.astype(jnp.float32),
        precision=lax.Precision.HIGHEST,
        preferred_element_type=jnp.float32,
    )
    early_input = shared_input + jnp.einsum(
        "st,sd->td",
        dispatch,
        input_back,
        precision=lax.Precision.HIGHEST,
        preferred_element_type=jnp.float32,
    )
    value_total, input_total = (
        lax.psum_scatter(early_value, "tensor", scatter_dimension=1, tiled=True),
        lax.psum_scatter(early_input, "tensor", scatter_dimension=1, tiled=True),
    )
    return (value_total.astype(jnp.bfloat16), input_total.astype(jnp.bfloat16))


def solution(mesh):
    in_specs = (
        P("expert", "tensor"),
        P("expert", "tensor"),
        P("expert", None),
        P("expert", None),
        P("tensor", None),
        P("tensor", None),
        P("tensor", None),
        P("expert", "tensor", None),
        P("expert", "tensor", None),
        P("expert", "tensor", None),
    )
    out_specs = (P("expert", "tensor"), P("expert", "tensor"))

    def layer(*args):
        fits = serves(dict(mesh.shape), args)
        program = jax.shard_map(
            paired if fits else on_device,
            mesh=mesh,
            in_specs=in_specs,
            out_specs=out_specs,
            check_vma=False,
        )
        return program(*args)

    return layer
```
